512 devices in a mesh: section: 32 (over z_hi, x, core), dp: 16 (over y, z_lo).
Axes of the slice: x: 4, y: 4, z: 16 (z_hi: 4, z_lo: 4; z = z_hi * 4 + z_lo), core: 2. Of those that a mesh axis runs over, the one named last changes fastest.
Arguments:
- saved_x: bfloat16 [2, 3, 32, 16, 16, 16, 128], P(None, None, 'section', 'dp'), may hold values from -6 to 6
- saved_h: bfloat16 [2, 3, 32, 16, 16, 16, 128], P(None, None, 'section', 'dp'), may hold values from -6 to 6
- kernels: bfloat16 [32, 2, 2, 9, 128, 128], P('section'), as said below
- grad_in: bfloat16 [2, 32, 16, 16, 16, 128], P(None, 'section', 'dp'), may hold values from -6 to 6
- loss_grads: bfloat16 [2, 2, 16, 16, 16, 128], P(None, None, 'dp'), may hold values from -6 to 6
Outputs:
- kernel_grads: float32 [32, 2304, 128], P('section', 'dp')
- edge_grads: bfloat16 [2, 32, 16, 16, 16, 128], P(None, 'section', 'dp')
The draws below stay inside these ranges and needn't reach their ends.
Inputs may be any that keep to these rules, and one draw needn't show every extreme that they name: kernels[d, 1] equals kernels[31 - d, 0]: each position holds replica 1's copy of the mirrored section. Every entry lies within 3 / sqrt(1152) in magnitude.
All inputs are finite; a program needn't handle non-finite values.
Results may differ from the reference program's by a relative error of at most 0.0052.
Values may be sent and summed in bfloat16 or wider, within the bound.
No kernel may reach another device: no remote copies, remote signals or barrier semaphores. Data moves between devices by JAX's collectives and lax.ppermute only.
A program may use at most 64 MiB of HBM per device.

```python
import jax
import jax.numpy as jnp
from jax import lax

C = 128
TILE = 16
TICKS = 3
SECTIONS = 32
BATCH = 16


def draw_kernels(key, part):
    base = jnp.clip(jax.random.normal(key, (SECTIONS, 2, 9, C, C), jnp.float32), -3.0, 3.0) * (9 * C) ** (-0.5)
    return jnp.stack([base, base[::-1]], axis=1).astype(jnp.bfloat16)


def shard_levels(rng, shape, cuts, low, top_value):
    level = 1.0
    for axis_at, blocks in cuts:
        steps = jax.random.uniform(jax.random.fold_in(jax.random.fold_in(rng, 6), axis_at), (blocks,), jnp.float32, low / len(cuts), top_value / len(cuts))
        level = level * jnp.repeat(jnp.exp(steps), shape[axis_at] // blocks).reshape((-1,) + (1,) * (len(shape) - 1 - axis_at))
    return level


def gaussian(stream_key, shape, width, bound, shards=(), dtype=jnp.bfloat16):
    result = jax.random.normal(stream_key, shape, jnp.float32) * width
    if len(shards) > 0:
        result = shard_levels(stream_key, shape, shards, -0.22, 0.18) * result
    return jnp.clip(result, min=-bound, max=bound).astype(dtype)


def setup_inputs(seed: int = 0) -> dict:
    key_list = jax.random.split(jax.random.key(seed), 6)
    saved_x = gaussian(key_list[0], (2, TICKS, SECTIONS, BATCH, TILE, TILE, C), 1.0, 6.0, ((2, 32), (3, 16)))
    saved_h = gaussian(key_list[1], (2, TICKS, SECTIONS, BATCH, TILE, TILE, C), 1.0, 6.0, ((2, 32), (3, 16)))
    kernels = draw_kernels(jax.random.fold_in(key_list[5], 71), 0)
    grad_in = gaussian(key_list[3], (2, SECTIONS, BATCH, TILE, TILE, C), 1.0, 6.0, ((1, 32), (2, 16)))
    loss_grads = gaussian(key_list[4], (2, TICKS - 1, BATCH, TILE, TILE, C), 1.0, 6.0, ((2, 16),))
    return dict(saved_x=saved_x, saved_h=saved_h, kernels=kernels, grad_in=grad_in, loss_grads=loss_grads)


highest = lax.Precision.HIGHEST


def tap_views(feature, sign):
    extent = feature.shape[1]
    padded = jnp.pad(feature, ((0, 0), (1, 1), (1, 1), (0, 0)))
    pieces = []
    for row_shift in (-1, 0, 1):
        for col_shift in (-1, 0, 1):
            row_start = 1 + sign * row_shift
            col_start = 1 + sign * col_shift
            pieces.append(padded[:, row_start:row_start + extent, col_start:col_start + extent, :])
    return jnp.stack(pieces, axis=3)


def block_back(grad_out, inputs, hidden, w_first, w_second):
    act_h = jnp.maximum(hidden, 0)
    act_x = jnp.maximum(inputs, 0)
    grad_z = jnp.einsum('byxkd,kcd->byxc', tap_views(grad_out, -1).astype(jnp.float32), w_second.astype(jnp.float32), precision=highest)
    g_second = jnp.einsum('byxkc,byxd->kcd', tap_views(act_h, 1).astype(jnp.float32), grad_out.astype(jnp.float32), precision=highest)
    grad_h = jnp.where(hidden > 0, grad_z, 0.0).astype(jnp.bfloat16)
    grad_u = jnp.einsum('byxkd,kcd->byxc', tap_views(grad_h, -1).astype(jnp.float32), w_first.astype(jnp.float32), precision=highest)
    g_first = jnp.einsum('byxkc,byxd->kcd', tap_views(act_x, 1).astype(jnp.float32), grad_h.astype(jnp.float32), precision=highest)
    grad_x = (grad_out.astype(jnp.float32) + jnp.where(inputs > 0, grad_u, 0.0)).astype(jnp.bfloat16)
    return grad_x, jnp.stack([g_first, g_second])


def section_back(pieces):
    return block_back(pieces[0], pieces[1], pieces[2], pieces[3], pieces[4])


def reference(saved_x, saved_h, kernels, grad_in, loss_grads):
    ticks_total = saved_x.shape[1]
    totals = [None, None]
    outgoing = None
    for tick_index in range(ticks_total):
        if tick_index == 0:
            incoming = [grad_in[0], grad_in[1]]
        else:
            incoming = [jnp.concatenate([outgoing[0][1:], loss_grads[0, tick_index - 1][None]], axis=0),
                        jnp.concatenate([loss_grads[1, tick_index - 1][None], outgoing[1][:-1]], axis=0)]
        new_out = []
        for replica in range(2):
            grad_x, grads = lax.map(section_back, (incoming[replica], saved_x[replica, tick_index], saved_h[replica, tick_index], kernels[:, replica, 0], kernels[:, replica, 1]))
            totals[replica] = grads if tick_index == 0 else totals[replica] + grads
            new_out.append(grad_x)
        outgoing = new_out
    summed = totals[0] + totals[1][::-1]
    extent = saved_x.shape[4]
    kernel_grads = (summed / float(extent * extent)).reshape(summed.shape[0], -1, summed.shape[-1])
    return kernel_grads, jnp.stack(outgoing)
```

```python
import functools

import jax
import jax.numpy as jnp
from jax import lax
from jax.experimental import pallas as pl
from jax.experimental.pallas import tpu as pltpu
from jax.sharding import PartitionSpec as P

TAPS = 9
PIECE = 64
VMEM_LIMIT = 16 << 20


def fill_shifts(pad_ref, value, extent):
    cells, channels = value.shape
    wide = value.astype(jnp.float32)
    column = lax.broadcasted_iota(jnp.int32, (cells, channels), 0) & (extent - 1)
    left = jnp.where(column == extent - 1, 0.0, pltpu.roll(wide, cells - 1, 0))
    right = jnp.where(column == 0, 0.0, pltpu.roll(wide, 1, 0))
    edge = jnp.zeros((extent, channels), value.dtype)
    for j, moved in enumerate((left.astype(value.dtype), value, right.astype(value.dtype))):
        pad_ref[j, 0:extent, :] = edge
        pad_ref[j, extent : extent + cells, :] = moved
        pad_ref[j, extent + cells : 2 * extent + cells, :] = edge


def views(pad_ref, extent):
    cells = pad_ref.shape[1] - 2 * extent
    taps = []
    for row in (-1, 0, 1):
        for col in (-1, 0, 1):
            start = (1 - row) * extent
            taps.append(pad_ref[col + 1, start : start + cells, :])
    return jnp.concatenate(taps, axis=1)


def conv_back(pad_ref, w_ref, replica, which, extent):
    weights = jnp.concatenate([w_ref[replica, which, k] for k in range(TAPS)], axis=1)
    return lax.dot_general(
        views(pad_ref, extent),
        weights,
        (((1,), (1,)), ((), ())),
        preferred_element_type=jnp.float32,
    )


def vmem():
    return pl.BlockSpec(memory_space=pltpu.VMEM)


def left_alone():
    return pl.BlockSpec(memory_space=pl.ANY)


def smem():
    return pl.BlockSpec(memory_space=pltpu.SMEM)


def chain_kernel(extent, tick, ticks, slot, packed, info_ref, x_ref, h_ref, w_ref, _, *refs):
    parity = info_ref[0]
    replica = parity if slot == 0 else 1 - parity
    refs = list(refs)
    pad_ref = refs.pop()
    if tick == 0:
        g = refs.pop(0)[replica]
    else:
        g = refs.pop(0)[...]
        if slot == 1:
            loss = refs.pop(0)[replica * (ticks - 1) + tick - 1]
            end = jnp.full(g.shape, info_ref[1], jnp.int32)
            g = jnp.where(end > 0, loss.astype(jnp.float32), g.astype(jnp.float32)).astype(g.dtype)
    first = refs.pop(0)[...] if packed else None
    gh_ref, gx_ref = refs[0], refs[1]
    if tick == 0 or slot == 1:
        refs[2][...] = g
    fill_shifts(pad_ref, g, extent)
    grad_z = conv_back(pad_ref, w_ref, replica, 1, extent)
    h = h_ref[replica * ticks + tick].astype(jnp.float32)
    grad_h = jnp.where(h > 0, grad_z, 0.0).astype(jnp.bfloat16)
    gh_ref[...] = grad_h
    fill_shifts(pad_ref, grad_h, extent)
    grad_u = conv_back(pad_ref, w_ref, replica, 0, extent)
    x = x_ref[replica * ticks + tick].astype(jnp.float32)
    grad_x = (g.astype(jnp.float32) + jnp.where(x > 0, grad_u, 0.0)).astype(jnp.bfloat16)
    if packed:
        gx_ref[replica] = grad_x
        gx_ref[1 - replica] = first
    else:
        gx_ref[...] = grad_x


def chain(info, saved_x, saved_h, weights, after, arrays, slot, tick, ticks, extent, packed):
    cells, channels = saved_x.shape[1:]
    like = jax.ShapeDtypeStruct((cells, channels), jnp.bfloat16)
    out_shape = [like, jax.ShapeDtypeStruct((2, cells, channels), jnp.bfloat16) if packed else like]
    if tick == 0 or slot == 1:
        out_shape.append(like)
    outs = pl.pallas_call(
        functools.partial(chain_kernel, extent, tick, ticks, slot, packed),
        in_specs=[smem()] + [vmem()] * 3 + [left_alone()] + [vmem()] * len(arrays),
        out_specs=[vmem()] * len(out_shape),
        out_shape=out_shape,
        scratch_shapes=[pltpu.VMEM((3, cells + 2 * extent, channels), jnp.bfloat16)],
        compiler_params=pltpu.CompilerParams(vmem_limit_bytes=VMEM_LIMIT),
        cost_estimate=pl.CostEstimate(
            flops=4 * cells * TAPS * channels * channels, bytes_accessed=1000000, transcendentals=0
        ),
        name=f"chain_{slot}_{tick}",
    )(info, saved_x, saved_h, weights, after, *arrays)
    return (outs[2] if len(outs) == 3 else arrays[0]), outs[0], outs[1]


def wgrad_kernel(extent, slot, ticks, at, has_acc, form, info_ref, x_ref, h_ref, *refs):
    parity = info_ref[0]
    replica = parity if slot == 0 else 1 - parity
    count = len(at)
    grads_h, grads = refs[:count], refs[count : 2 * count]
    acc_ref = refs[2 * count] if has_acc else None
    out_ref, pad_ref = refs[-2], refs[-1]
    if form == "both":
        out_ref[:, 0] = refs[2 * count + 1][...]
    for pair, (act_ref, sides) in enumerate(((x_ref, grads_h), (h_ref, grads))):
        rows, columns = [], []
        for n, tick in enumerate(at):
            fill_shifts(pad_ref.at[pair, n], sides[n][...], extent)
            columns.append(views(pad_ref.at[pair, n], extent))
            act = act_ref[replica * ticks + tick].astype(jnp.float32)
            rows.append(jnp.maximum(act, 0.0).astype(jnp.bfloat16))
        left = rows[0] if count == 1 else jnp.concatenate(rows, axis=0)
        right = columns[0] if count == 1 else jnp.concatenate(columns, axis=0)
        total = lax.dot_general(
            left, right, (((0,), (0,)), ((), ())), preferred_element_type=jnp.float32
        )
        channels = left.shape[1]
        for k in range(TAPS):
            for start in range(0, channels, PIECE):
                piece = total[start : start + PIECE, k * channels : (k + 1) * channels]
                row = (pair * TAPS + k) * channels + start
                if has_acc:
                    piece = piece + acc_ref[row : row + PIECE, :]
                if form == "flat":
                    out_ref[row : row + PIECE, :] = piece
                    continue
                rows_each = out_ref.shape[-2]
                part, inner = row // rows_each, row % rows_each
                at_part = (part, slot) if form == "both" else (part,)
                out_ref[*at_part, inner : inner + PIECE, :] = piece.astype(out_ref.dtype)


def wgrad(info, saved_x, saved_h, grads_h, grads, at, more, slot, ticks, extent, parts, form):
    cells, channels = saved_x.shape[1:]
    rows = 2 * TAPS * channels
    shape = {
        "flat": (rows, channels),
        "parts": (parts, rows // parts, channels),
        "both": (parts, 2, rows // parts, channels),
    }[form]
    out_shape = jax.ShapeDtypeStruct(shape, jnp.float32 if form == "flat" else jnp.bfloat16)
    args = [*grads_h, *grads, *more]
    return pl.pallas_call(
        functools.partial(wgrad_kernel, extent, slot, ticks, at, len(more) > 0, form),
        in_specs=[smem()] + [vmem()] * (2 + len(args)),
        out_specs=vmem(),
        out_shape=out_shape,
        scratch_shapes=[pltpu.VMEM((2, len(at), 3, cells + 2 * extent, channels), jnp.bfloat16)],
        compiler_params=pltpu.CompilerParams(vmem_limit_bytes=VMEM_LIMIT),
        cost_estimate=pl.CostEstimate(
            flops=4 * len(at) * cells * TAPS * channels * channels,
            bytes_accessed=2000000,
            transcendentals=0,
        ),
        name=f"wgrad_{slot}_" + "".join(str(t) for t in at),
    )(info, saved_x, saved_h, *args)


def exchange(value, offset):
    total = lax.axis_size("section")
    pairs = []
    for low in range(offset, total - 1, 2):
        pairs += [(low, low + 1), (low + 1, low)]
    return lax.ppermute(value, "section", pairs)


def on_device(factors, saved_x, saved_h, kernels, grad_in, loss_grads):
    ticks = saved_x.shape[1]
    extent, channels = saved_x.shape[4], saved_x.shape[6]
    cells = extent * extent
    sections = lax.axis_size("section")
    outer, inner = factors
    position = lax.axis_index("section")
    parity = position % 2
    at_end = (position == 0) | (position == sections - 1)
    info = jnp.stack([parity, at_end.astype(jnp.int32)]).astype(jnp.int32)
    weights = kernels[0]
    xs = saved_x.reshape(-1, cells, channels)
    hs = saved_h.reshape(-1, cells, channels)
    start = grad_in.reshape(-1, cells, channels)
    loss = loss_grads.reshape(-1, cells, channels)

    run = functools.partial(chain, info, xs, hs, weights, ticks=ticks, extent=extent)
    sums = functools.partial(wgrad, info, xs, hs, ticks=ticks, extent=extent, parts=outer)
    g, gh = [[], []], [[], []]
    arrivals = [None, None]
    out = [None, None]
    after = start
    for tick in range(ticks):
        last = tick == ticks - 1
        for slot in (0, 1):
            if tick == 0:
                arrays = [start]
            elif slot == 0:
                arrays = [arrivals[0]]
            else:
                arrays = [arrivals[1], loss]
            packed = last and slot == 1
            if packed:
                slot0 = sums(gh[0], g[0], tuple(range(ticks)), [], slot=0, form="parts")
                after = slot0
                arrays.append(out[0])
            g_now, gh_now, out[slot] = run(after, arrays, slot=slot, tick=tick, packed=packed)
            after = gh_now
            g[slot].append(g_now)
            gh[slot].append(gh_now)
            if not last:
                if slot == 0:
                    next_one = exchange(out[0], 1)
                else:
                    arrivals = [exchange(out[1], 0), next_one]
    edge_grads = out[1].reshape(2, 1, 1, extent, extent, channels)

    early = tuple(range(ticks - 1))
    part1 = sums(gh[1][:-1], g[1][:-1], early, [], slot=1, form="flat")
    both = sums(gh[1][-1:], g[1][-1:], (ticks - 1,), [part1, slot0], slot=1, form="both")

    rows = both.shape[2]
    across = [[i * inner + j for i in range(outer)] for j in range(inner)]
    along = [[i * inner + j for j in range(inner)] for i in range(outer)]

    def total(value):
        parts = [value[n].astype(jnp.float32) for n in range(value.shape[0])]
        return functools.reduce(lambda a, b: a + b, parts)

    both = lax.all_to_all(both, "dp", 0, 0, axis_index_groups=across, tiled=True)
    summed = total(both)
    mine = jnp.where(parity == 0, summed[0], summed[1]).astype(jnp.bfloat16)
    other = jnp.where(parity == 0, summed[1], summed[0]).astype(jnp.bfloat16)

    def finish(value):
        value = value.reshape(inner, rows // inner, channels)
        return total(lax.all_to_all(value, "dp", 0, 0, axis_index_groups=along, tiled=True))

    other = finish(other).astype(jnp.bfloat16)
    mirror = [(i, sections - 1 - i) for i in range(sections)]
    other = lax.ppermute(other, "section", mirror)
    mine = finish(mine)
    factor = 1.0 / float(cells)
    kernel_grads = ((mine + other.astype(jnp.float32)) * factor)[None]
    return (kernel_grads, edge_grads)


def solution(mesh):
    shards = mesh.shape["dp"]
    outer = next(f for f in (4, 2, 1) if shards % f == 0)
    return jax.shard_map(
        functools.partial(on_device, (outer, shards // outer)),
        mesh=mesh,
        in_specs=(
            P(None, None, "section", "dp", None, None, None),
            P(None, None, "section", "dp", None, None, None),
            P("section", None, None, None, None, None),
            P(None, "section", "dp", None, None, None),
            P(None, None, "dp", None, None, None),
        ),
        out_specs=(P("section", "dp", None), P(None, "section", "dp", None, None, None)),
        check_vma=False,
    )
```

```python
import functools

import jax
import jax.numpy as jnp
from jax import lax
from jax.experimental import pallas as pl
from jax.experimental.pallas import tpu as pltpu
from jax.sharding import PartitionSpec as P


TAPS = 9
PIECE = 64
PARAMS = pltpu.CompilerParams(vmem_limit_bytes=16 << 20)
BF16, F32 = jnp.bfloat16, jnp.float32


def fill_shifts(pad_ref, value, extent):
    cells, channels = value.shape
    wide = value.astype(F32)
    column = lax.broadcasted_iota(jnp.int32, (cells, channels), 0) & (extent - 1)
    left = jnp.where(column == extent - 1, 0.0, pltpu.roll(wide, cells - 1, 0))
    right = jnp.where(column == 0, 0.0, pltpu.roll(wide, 1, 0))
    edge = jnp.zeros((extent, channels), value.dtype)
    for j, moved in enumerate((left.astype(value.dtype), value, right.astype(value.dtype))):
        pad_ref[j, 0:extent, :] = edge
        pad_ref[j, extent : extent + cells, :] = moved
        pad_ref[j, extent + cells : 2 * extent + cells, :] = edge


def views(pad_ref, extent):
    cells = pad_ref.shape[1] - 2 * extent
    taps = []
    for row in (-1, 0, 1):
        for col in (-1, 0, 1):
            start = (1 - row) * extent
            taps.append(pad_ref[col + 1, start : start + cells, :])
    return jnp.concatenate(taps, axis=1)


def conv_back(pad_ref, w_ref, extent):
    weights = jnp.concatenate([w_ref[k] for k in range(TAPS)], axis=1)
    return lax.dot_general(
        views(pad_ref, extent), weights, (((1,), (1,)), ((), ())), preferred_element_type=F32
    )


def step(g, x_ref, h_ref, w_ref, pad_g, pad_gh, extent):
    fill_shifts(pad_g, g, extent)
    grad_z = conv_back(pad_g, w_ref.at[1], extent)
    grad_h = jnp.where(h_ref[...].astype(F32) > 0, grad_z, 0.0).astype(BF16)
    fill_shifts(pad_gh, grad_h, extent)
    grad_u = conv_back(pad_gh, w_ref.at[0], extent)
    moved = jnp.where(x_ref[...].astype(F32) > 0, grad_u, 0.0)
    return grad_h, (g.astype(F32) + moved).astype(BF16)


def kernel_sums(act_refs, pads, extent):
    rows = [jnp.maximum(a[...].astype(F32), 0.0).astype(BF16) for a in act_refs]
    columns = [views(pad, extent) for pad in pads]
    return lax.dot_general(
        jnp.concatenate(rows, axis=0),
        jnp.concatenate(columns, axis=0),
        (((0,), (0,)), ((), ())),
        preferred_element_type=F32,
    )


def pieces(total, pair):
    channels = total.shape[0]
    for k in range(TAPS):
        for start in range(0, channels, PIECE):
            row = (pair * TAPS + k) * channels + start
            yield row, total[start : start + PIECE, k * channels : (k + 1) * channels]


def first_kernel(extent, ticks, x_hbm, h_hbm, w_hbm, g_hbm, l_hbm, *refs):
    xs, hs, ws, loss, g0, g1, gh0, gh1, gx0, gx1, pads, sems = refs
    gs = (g0, g1)
    position = lax.axis_index("section")
    parity = position & 1
    at_end = (position == 0) | (position == lax.axis_size("section") - 1)
    copies = []

    def fetch(source, target):
        copy = pltpu.make_async_copy(source, target, sems.at[len(copies)])
        copy.start()
        copies.append(copy)

    for slot in (0, 1):
        replica = parity if slot == 0 else 1 - parity
        fetch(g_hbm.at[replica], gs[slot])
        fetch(w_hbm.at[replica, 1], ws.at[slot, 1])
        fetch(h_hbm.at[pl.ds(replica * ticks, ticks)], hs.at[slot])
        fetch(w_hbm.at[replica, 0], ws.at[slot, 0])
        fetch(x_hbm.at[pl.ds(replica * ticks, ticks)], xs.at[slot])
    fetch(l_hbm.at[pl.ds((1 - parity) * (ticks - 1), ticks - 1)], loss)
    for slot, gh_ref, gx_ref in ((0, gh0, gx0), (1, gh1, gx1)):
        for copy in copies[5 * slot : 5 * slot + 5]:
            copy.wait()
        gh_ref[...], gx_ref[...] = step(
            gs[slot][...], xs.at[slot, 0], hs.at[slot, 0], ws.at[slot], pads.at[0], pads.at[1], extent
        )
    copies[-1].wait()

    @pl.when(jnp.logical_not(at_end))
    def _():
        loss[...] = jnp.zeros_like(loss)


def middle_kernel(extent, slot, tick, x_ref, h_ref, w_ref, g_ref, *refs):
    pads = refs[-1]
    g = g_ref[...]
    if slot == 1:
        loss_ref, gh_ref, gx_ref, used_ref = refs[:-1]
        g = (g.astype(F32) + loss_ref[tick - 1].astype(F32)).astype(BF16)
        used_ref[...] = g
    else:
        gh_ref, gx_ref = refs[:-1]
    gh_ref[...], gx_ref[...] = step(
        g,
        x_ref.at[slot, tick],
        h_ref.at[slot, tick],
        w_ref.at[slot],
        pads.at[0],
        pads.at[1],
        extent,
    )


def sums_kernel(extent, ticks, x_ref, h_ref, *refs):
    grads_h, grads = refs[:ticks], refs[ticks : 2 * ticks]
    out_ref, pads = refs[2 * ticks :]
    for pair, (act_ref, sides) in enumerate(((x_ref, grads_h), (h_ref, grads))):
        for n in range(ticks):
            fill_shifts(pads.at[pair, n], sides[n][...], extent)
        acts = [act_ref.at[0, n] for n in range(ticks)]
        total = kernel_sums(acts, [pads.at[pair, n] for n in range(ticks)], extent)
        for row, value in pieces(total, pair):
            out_ref[row : row + PIECE, :] = value.astype(BF16)


def last_kernel(extent, ticks, x_ref, h_ref, w_ref, g_ref, loss_ref, gx0_ref, sums0_ref, *refs):
    early = ticks - 1
    grads_h, grads = refs[:early], refs[early : 2 * early]
    edge_ref, out_ref, pads = refs[2 * early :]
    parity = lax.axis_index("section") & 1
    replica = 1 - parity
    g = (g_ref[...].astype(F32) + loss_ref[early - 1].astype(F32)).astype(BF16)
    _, grad_x = step(
        g,
        x_ref.at[1, early],
        h_ref.at[1, early],
        w_ref.at[1],
        pads.at[1, early],
        pads.at[0, early],
        extent,
    )
    edge_ref[replica] = grad_x
    edge_ref[parity] = gx0_ref[...]
    rows_each = out_ref.shape[2]
    for part in range(out_ref.shape[0]):
        out_ref[part, parity] = sums0_ref[part * rows_each : (part + 1) * rows_each, :]
    for pair, (act_ref, sides) in enumerate(((x_ref, grads_h), (h_ref, grads))):
        for n in range(early):
            fill_shifts(pads.at[pair, n], sides[n][...], extent)
        acts = [act_ref.at[1, n] for n in range(ticks)]
        total = kernel_sums(acts, [pads.at[pair, n] for n in range(ticks)], extent)
        for row, value in pieces(total, pair):
            part, inner = row // rows_each, row % rows_each
            out_ref[part, replica, inner : inner + PIECE, :] = value.astype(BF16)


def call(body, steps, in_specs, out_shape, scratch, args):
    cells, channels = args[0].shape[-2:]
    return pl.pallas_call(
        body,
        in_specs=in_specs,
        out_specs=[vmem()] * len(out_shape),
        out_shape=out_shape,
        scratch_shapes=scratch,
        compiler_params=PARAMS,
        cost_estimate=pl.CostEstimate(
            flops=4 * steps * cells * TAPS * channels * channels,
            bytes_accessed=1000000,
            transcendentals=0,
        ),
    )(*args)


def vmem():
    return pl.BlockSpec(memory_space=pltpu.VMEM)


def in_hbm():
    return pl.BlockSpec(memory_space=pltpu.HBM)


def exchange(value, offset):
    total = lax.axis_size("section")
    pairs = []
    for low in range(offset, total - 1, 2):
        pairs += [(low, low + 1), (low + 1, low)]
    return lax.ppermute(value, "section", pairs)


def on_device(factors, saved_x, saved_h, kernels, grad_in, loss_grads):
    return whole(factors, saved_x, saved_h, kernels, grad_in, loss_grads)


def whole(factors, saved_x, saved_h, kernels, grad_in, loss_grads):
    ticks = saved_x.shape[1]
    extent, channels = saved_x.shape[4], saved_x.shape[6]
    cells = extent * extent
    sections = lax.axis_size("section")
    outer, inner = factors
    rows = 2 * TAPS * channels
    field = (cells, channels)

    def shape(*lead, tail=field):
        return jax.ShapeDtypeStruct((*lead, *tail), BF16)

    def pads(*lead):
        return pltpu.VMEM((*lead, 3, cells + 2 * extent, channels), BF16)

    xs, hs, ws, loss, g0, g1, gh0, gh1, out0, out1 = call(
        functools.partial(first_kernel, extent, ticks),
        2,
        [in_hbm()] * 5,
        [
            shape(2, ticks),
            shape(2, ticks),
            shape(*kernels.shape[1:-2], tail=(channels, channels)),
            shape(ticks - 1),
            *[shape()] * 6,
        ],
        [pads(2), pltpu.SemaphoreType.DMA((11,))],
        [
            pltpu.with_memory_space_constraint(value, pltpu.HBM)
            for value in (
                saved_x.reshape(-1, *field),
                saved_h.reshape(-1, *field),
                kernels[0],
                grad_in.reshape(-1, *field),
                loss_grads.reshape(-1, *field),
            )
        ],
    )
    g, gh = [[g0], [g1]], [[gh0], [gh1]]
    for tick in range(1, ticks):
        far = exchange(out0, 1)
        near = exchange(out1, 0)
        gh0, out0 = call(
            functools.partial(middle_kernel, extent, 0, tick),
            1,
            [vmem()] * 4,
            [shape(), shape()],
            [pads(2)],
            (xs, hs, ws, near),
        )
        g[0].append(near)
        gh[0].append(gh0)
        if tick < ticks - 1:
            gh1, out1, g1 = call(
                functools.partial(middle_kernel, extent, 1, tick),
                1,
                [vmem()] * 5,
                [shape(), shape(), shape()],
                [pads(2)],
                (xs, hs, ws, far, loss),
            )
            g[1].append(g1)
            gh[1].append(gh1)
    (sums0,) = call(
        functools.partial(sums_kernel, extent, ticks),
        ticks,
        [vmem()] * (2 + 2 * ticks),
        [shape(tail=(rows, channels))],
        [pads(2, ticks)],
        (xs, hs, *gh[0], *g[0]),
    )
    edge, both = call(
        functools.partial(last_kernel, extent, ticks),
        1 + ticks,
        [vmem()] * (7 + 2 * (ticks - 1)),
        [shape(2), shape(outer, 2, rows // outer, tail=(channels,))],
        [pads(2, ticks)],
        (xs, hs, ws, far, loss, out0, sums0, *gh[1], *g[1]),
    )
    edge_grads = edge.reshape(2, 1, 1, extent, extent, channels)

    across = [[i * inner + j for i in range(outer)] for j in range(inner)]
    along = [[i * inner + j for j in range(inner)] for i in range(outer)]

    def total(value):
        parts = [value[n].astype(F32) for n in range(value.shape[0])]
        return functools.reduce(lambda a, b: a + b, parts)

    def spread(value, groups):
        return lax.all_to_all(value, "dp", 0, 0, axis_index_groups=groups, tiled=True)

    both = spread(both, across)

    def finish(replica):
        value = total(both[:, replica]).astype(BF16)
        value = value.reshape(inner, rows // outer // inner, channels)
        value = spread(value, along)
        return total(value)

    other = finish(1).astype(BF16)
    other = lax.ppermute(other, "section", [(i, sections - 1 - i) for i in range(sections)])
    mine = finish(0)
    kernel_grads = ((mine + other.astype(F32)) * (1.0 / float(cells)))[None]
    return (kernel_grads, edge_grads)


def solution(mesh):
    shards = mesh.shape["dp"]
    outer = next(f for f in (4, 2, 1) if shards % f == 0)
    return jax.shard_map(
        functools.partial(on_device, (outer, shards // outer)),
        mesh=mesh,
        in_specs=(
            P(None, None, "section", "dp", None, None, None),
            P(None, None, "section", "dp", None, None, None),
            P("section", None, None, None, None, None),
            P(None, "section", "dp", None, None, None),
            P(None, None, "dp", None, None, None),
        ),
        out_specs=(P("section", "dp", None), P(None, "section", "dp", None, None, None)),
        check_vma=False,
    )
```

```python
import functools

import jax
import jax.numpy as jnp
from jax import lax
from jax.experimental import pallas as pl
from jax.experimental.pallas import tpu as pltpu
from jax.sharding import PartitionSpec as P


TAPS = 9
PIECE = 16
PARAMS = pltpu.CompilerParams(vmem_limit_bytes=16 << 20)
BF16, F32 = jnp.bfloat16, jnp.float32


def fill_shifts(pad_ref, value, extent):
    cells, channels = value.shape
    wide = value.astype(F32)
    column = lax.broadcasted_iota(jnp.int32, (cells, channels), 0) & (extent - 1)
    left = jnp.where(column == extent - 1, 0.0, pltpu.roll(wide, cells - 1, 0))
    right = jnp.where(column == 0, 0.0, pltpu.roll(wide, 1, 0))
    edge = jnp.zeros((extent, channels), value.dtype)
    for j, moved in enumerate((left.astype(value.dtype), value, right.astype(value.dtype))):
        pad_ref[j, 0:extent, :] = edge
        pad_ref[j, extent : extent + cells, :] = moved
        pad_ref[j, extent + cells : 2 * extent + cells, :] = edge


def views(pad_ref, extent):
    cells = pad_ref.shape[1] - 2 * extent
    taps = []
    for row in (-1, 0, 1):
        for col in (-1, 0, 1):
            start = (1 - row) * extent
            taps.append(pad_ref[col + 1, start : start + cells, :])
    return jnp.concatenate(taps, axis=1)


def conv_back(pad_ref, w_ref, extent):
    weights = jnp.concatenate([w_ref[k] for k in range(TAPS)], axis=1)
    return lax.dot_general(
        views(pad_ref, extent), weights, (((1,), (1,)), ((), ())), preferred_element_type=F32
    )


def step(g, x_ref, h_ref, w_ref, pad_g, pad_gh, extent):
    fill_shifts(pad_g, g, extent)
    grad_z = conv_back(pad_g, w_ref.at[1], extent)
    grad_h = jnp.where(h_ref[...].astype(F32) > 0, grad_z, 0.0).astype(BF16)
    fill_shifts(pad_gh, grad_h, extent)
    grad_u = conv_back(pad_gh, w_ref.at[0], extent)
    moved = jnp.where(x_ref[...].astype(F32) > 0, grad_u, 0.0)
    return grad_h, (g.astype(F32) + moved).astype(BF16)


def kernel_sums(act_refs, pads, extent):
    rows = [jnp.maximum(a[...].astype(F32), 0.0).astype(BF16) for a in act_refs]
    columns = [views(pad, extent) for pad in pads]
    return lax.dot_general(
        jnp.concatenate(rows, axis=0),
        jnp.concatenate(columns, axis=0),
        (((0,), (0,)), ((), ())),
        preferred_element_type=F32,
    )


def pieces(total, pair):
    channels = total.shape[0]
    for k in range(TAPS):
        for start in range(0, channels, PIECE):
            row = (pair * TAPS + k) * channels + start
            yield row, total[start : start + PIECE, k * channels : (k + 1) * channels]


def first_kernel(extent, ticks, x_hbm, h_hbm, w_hbm, g_hbm, l_hbm, *refs):
    xs, hs, ws, loss, g0, g1, gh0, gh1, gx0, gx1, pads, sems = refs
    gs = (g0, g1)
    position = lax.axis_index("section")
    parity = position & 1
    at_end = (position == 0) | (position == lax.axis_size("section") - 1)
    copies = []

    def fetch(source, target):
        copy = pltpu.make_async_copy(source, target, sems.at[len(copies)])
        copy.start()
        copies.append(copy)

    for slot in (0, 1):
        replica = parity if slot == 0 else 1 - parity
        fetch(g_hbm.at[replica], gs[slot])
        fetch(w_hbm.at[replica, 1], ws.at[slot, 1])
        fetch(h_hbm.at[pl.ds(replica * ticks, ticks)], hs.at[slot])
        fetch(w_hbm.at[replica, 0], ws.at[slot, 0])
        fetch(x_hbm.at[pl.ds(replica * ticks, ticks)], xs.at[slot])
    fetch(l_hbm.at[pl.ds((1 - parity) * (ticks - 1), ticks - 1)], loss)
    for slot, gh_ref, gx_ref in ((0, gh0, gx0), (1, gh1, gx1)):
        for copy in copies[5 * slot : 5 * slot + 5]:
            copy.wait()
        gh_ref[...], gx_ref[...] = step(
            gs[slot][...], xs.at[slot, 0], hs.at[slot, 0], ws.at[slot], pads.at[0], pads.at[1], extent
        )
    copies[-1].wait()

    @pl.when(jnp.logical_not(at_end))
    def _():
        loss[...] = jnp.zeros_like(loss)


def middle_kernel(extent, slot, tick, x_ref, h_ref, w_ref, g_ref, *refs):
    pads = refs[-1]
    g = g_ref[...]
    if slot == 1:
        loss_ref, gh_ref, gx_ref, used_ref = refs[:-1]
        g = (g.astype(F32) + loss_ref[tick - 1].astype(F32)).astype(BF16)
        used_ref[...] = g
    else:
        gh_ref, gx_ref = refs[:-1]
    gh_ref[...], gx_ref[...] = step(
        g,
        x_ref.at[slot, tick],
        h_ref.at[slot, tick],
        w_ref.at[slot],
        pads.at[0],
        pads.at[1],
        extent,
    )


def sums_kernel(extent, ticks, x_ref, h_ref, *refs):
    grads_h, grads = refs[:ticks], refs[ticks : 2 * ticks]
    out_ref, pads = refs[2 * ticks :]
    for pair, (act_ref, sides) in enumerate(((x_ref, grads_h), (h_ref, grads))):
        for n in range(ticks):
            fill_shifts(pads.at[pair, n], sides[n][...], extent)
        acts = [act_ref.at[0, n] for n in range(ticks)]
        total = kernel_sums(acts, [pads.at[pair, n] for n in range(ticks)], extent)
        for row, value in pieces(total, pair):
            out_ref[row : row + PIECE, :] = value.astype(BF16)


def last_kernel(extent, ticks, parts, x_ref, h_ref, w_ref, g_ref, loss_ref, gx0_ref, sums0_ref, *refs):
    early = ticks - 1
    grads_h, grads = refs[:early], refs[early : 2 * early]
    edge_ref, out_ref, pads = refs[2 * early :]
    position = lax.axis_index("section")
    parity = position & 1
    replica = 1 - parity
    g = (g_ref[...].astype(F32) + loss_ref[early - 1].astype(F32)).astype(BF16)
    _, grad_x = step(
        g,
        x_ref.at[1, early],
        h_ref.at[1, early],
        w_ref.at[1],
        pads.at[1, early],
        pads.at[0, early],
        extent,
    )
    edge_ref[replica] = grad_x
    edge_ref[parity] = gx0_ref[...]
    members, _, later, rows_each, _ = out_ref.shape
    upper = (position >= lax.axis_size("section") // 2).astype(jnp.int32)
    half0, half1 = (parity + upper) & 1, (replica + upper) & 1

    def put(row, half, value):
        shard, inner = row // rows_each, row % rows_each
        block, pair_at = shard // (2 * later), shard % (2 * later)
        member = block * (members // parts) + pair_at % 2
        out_ref[member, half, pair_at // 2, inner : inner + value.shape[0], :] = value

    for row in range(0, sums0_ref.shape[0], rows_each):
        put(row, half0, sums0_ref[row : row + rows_each, :])
    for pair, (act_ref, sides) in enumerate(((x_ref, grads_h), (h_ref, grads))):
        for n in range(early):
            fill_shifts(pads.at[pair, n], sides[n][...], extent)
        acts = [act_ref.at[1, n] for n in range(ticks)]
        total = kernel_sums(acts, [pads.at[pair, n] for n in range(ticks)], extent)
        for row, value in pieces(total, pair):
            put(row, half1, value.astype(BF16))


def call(body, steps, in_specs, out_shape, scratch, args):
    cells, channels = args[0].shape[-2:]
    return pl.pallas_call(
        body,
        in_specs=in_specs,
        out_specs=[vmem()] * len(out_shape),
        out_shape=out_shape,
        scratch_shapes=scratch,
        compiler_params=PARAMS,
        cost_estimate=pl.CostEstimate(
            flops=4 * steps * cells * TAPS * channels * channels,
            bytes_accessed=1000000,
            transcendentals=0,
        ),
    )(*args)


def vmem():
    return pl.BlockSpec(memory_space=pltpu.VMEM)


def in_hbm():
    return pl.BlockSpec(memory_space=pltpu.HBM)


def exchange(value, offset):
    total = lax.axis_size("section")
    pairs = []
    for low in range(offset, total - 1, 2):
        pairs += [(low, low + 1), (low + 1, low)]
    return lax.ppermute(value, "section", pairs)


def on_device(factors, saved_x, saved_h, kernels, grad_in, loss_grads):
    return whole(factors, saved_x, saved_h, kernels, grad_in, loss_grads)


def whole(factors, saved_x, saved_h, kernels, grad_in, loss_grads):
    ticks = saved_x.shape[1]
    extent, channels = saved_x.shape[4], saved_x.shape[6]
    cells = extent * extent
    sections = lax.axis_size("section")
    outer, inner = factors
    later, shards = inner // 2, outer * inner
    rows = 2 * TAPS * channels
    field = (cells, channels)

    def shape(*lead, tail=field):
        return jax.ShapeDtypeStruct((*lead, *tail), BF16)

    def pads(*lead):
        return pltpu.VMEM((*lead, 3, cells + 2 * extent, channels), BF16)

    xs, hs, ws, loss, g0, g1, gh0, gh1, out0, out1 = call(
        functools.partial(first_kernel, extent, ticks),
        2,
        [in_hbm()] * 5,
        [
            shape(2, ticks),
            shape(2, ticks),
            shape(*kernels.shape[1:-2], tail=(channels, channels)),
            shape(ticks - 1),
            *[shape()] * 6,
        ],
        [pads(2), pltpu.SemaphoreType.DMA((11,))],
        [
            pltpu.with_memory_space_constraint(value, pltpu.HBM)
            for value in (
                saved_x.reshape(-1, *field),
                saved_h.reshape(-1, *field),
                kernels[0],
                grad_in.reshape(-1, *field),
                loss_grads.reshape(-1, *field),
            )
        ],
    )
    g, gh = [[g0], [g1]], [[gh0], [gh1]]
    for tick in range(1, ticks):
        far = exchange(out0, 1)
        near = exchange(out1, 0)
        gh0, out0 = call(
            functools.partial(middle_kernel, extent, 0, tick),
            1,
            [vmem()] * 4,
            [shape(), shape()],
            [pads(2)],
            (xs, hs, ws, near),
        )
        g[0].append(near)
        gh[0].append(gh0)
        if tick < ticks - 1:
            gh1, out1, g1 = call(
                functools.partial(middle_kernel, extent, 1, tick),
                1,
                [vmem()] * 5,
                [shape(), shape(), shape()],
                [pads(2)],
                (xs, hs, ws, far, loss),
            )
            g[1].append(g1)
            gh[1].append(gh1)
    (sums0,) = call(
        functools.partial(sums_kernel, extent, ticks),
        ticks,
        [vmem()] * (2 + 2 * ticks),
        [shape(tail=(rows, channels))],
        [pads(2, ticks)],
        (xs, hs, *gh[0], *g[0]),
    )
    edge, both = call(
        functools.partial(last_kernel, extent, ticks, outer),
        1 + ticks,
        [vmem()] * (7 + 2 * (ticks - 1)),
        [shape(2), shape(2 * outer, 2, later, rows // shards, tail=(channels,))],
        [pads(2, ticks)],
        (xs, hs, ws, far, loss, out0, sums0, *gh[1], *g[1]),
    )
    edge_grads = edge.reshape(2, 1, 1, extent, extent, channels)

    def shard(block, far, near):
        return (block * later + far) * 2 + near

    first_groups = [
        [shard(block, far, near) for block in range(outer) for near in range(2)]
        for far in range(later)
    ]
    second_groups = [
        [
            section * shards + shard(block, far, near)
            for section in (low, sections - 1 - low)
            for far in range(later)
        ]
        for low in range(sections // 2)
        for block in range(outer)
        for near in range(2)
    ]

    def total(value):
        parts = [value[n].astype(F32) for n in range(value.shape[0])]
        return functools.reduce(lambda a, b: a + b, parts)

    both = lax.all_to_all(both, "dp", 0, 0, axis_index_groups=first_groups, tiled=True)
    both = total(both).astype(BF16).reshape(2 * later, rows // shards, channels)
    both = lax.all_to_all(
        both, ("section", "dp"), 0, 0, axis_index_groups=second_groups, tiled=True
    )
    kernel_grads = (total(both) * (1.0 / float(cells)))[None]
    return (kernel_grads, edge_grads)


def solution(mesh):
    shards = mesh.shape["dp"]
    outer = next(f for f in (4, 2, 1) if shards % f == 0)
    return jax.shard_map(
        functools.partial(on_device, (outer, shards // outer)),
        mesh=mesh,
        in_specs=(
            P(None, None, "section", "dp", None, None, None),
            P(None, None, "section", "dp", None, None, None),
            P("section", None, None, None, None, None),
            P(None, "section", "dp", None, None, None),
            P(None, None, "dp", None, None, None),
        ),
        out_specs=(P("section", "dp", None), P(None, "section", "dp", None, None, None)),
        check_vma=False,
    )
```

```python
import functools

import jax
import jax.numpy as jnp
from jax import lax
from jax.experimental import pallas as pl
from jax.experimental.pallas import tpu as pltpu
from jax.sharding import PartitionSpec as P


TAPS = 9
PIECE = 16
PARAMS = pltpu.CompilerParams(vmem_limit_bytes=16 << 20)
BF16, F32 = jnp.bfloat16, jnp.float32


def fill_shifts(pad_ref, value, extent):
    cells, channels = value.shape
    wide = value.astype(F32)
    column = lax.broadcasted_iota(jnp.int32, (cells, channels), 0) & (extent - 1)
    left = jnp.where(column == extent - 1, 0.0, pltpu.roll(wide, cells - 1, 0))
    right = jnp.where(column == 0, 0.0, pltpu.roll(wide, 1, 0))
    edge = jnp.zeros((extent, channels), value.dtype)
    for j, moved in enumerate((left.astype(value.dtype), value, right.astype(value.dtype))):
        pad_ref[j, 0:extent, :] = edge
        pad_ref[j, extent : extent + cells, :] = moved
        pad_ref[j, extent + cells : 2 * extent + cells, :] = edge


def views(pad_ref, extent):
    cells = pad_ref.shape[1] - 2 * extent
    taps = []
    for row in (-1, 0, 1):
        for col in (-1, 0, 1):
            start = (1 - row) * extent
            taps.append(pad_ref[col + 1, start : start + cells, :])
    return jnp.concatenate(taps, axis=1)


def conv_back(pad_ref, w_ref, extent):
    weights = jnp.concatenate([w_ref[k] for k in range(TAPS)], axis=1)
    return lax.dot_general(
        views(pad_ref, extent), weights, (((1,), (1,)), ((), ())), preferred_element_type=F32
    )


def step(g, x_ref, h_ref, w_ref, pad_g, pad_gh, extent):
    fill_shifts(pad_g, g, extent)
    grad_z = conv_back(pad_g, w_ref.at[1], extent)
    grad_h = jnp.where(h_ref[...].astype(F32) > 0, grad_z, 0.0).astype(BF16)
    fill_shifts(pad_gh, grad_h, extent)
    grad_u = conv_back(pad_gh, w_ref.at[0], extent)
    moved = jnp.where(x_ref[...].astype(F32) > 0, grad_u, 0.0)
    return grad_h, (g.astype(F32) + moved).astype(BF16)


def kernel_sums(act_refs, pads, extent):
    rows = [jnp.maximum(a[...].astype(F32), 0.0).astype(BF16) for a in act_refs]
    columns = [views(pad, extent) for pad in pads]
    return lax.dot_general(
        jnp.concatenate(rows, axis=0),
        jnp.concatenate(columns, axis=0),
        (((0,), (0,)), ((), ())),
        preferred_element_type=F32,
    )


def pieces(total, pair):
    channels = total.shape[0]
    for k in range(TAPS):
        for start in range(0, channels, PIECE):
            row = (pair * TAPS + k) * channels + start
            yield row, total[start : start + PIECE, k * channels : (k + 1) * channels]


def first_kernel(extent, ticks, x_hbm, h_hbm, w_hbm, g_hbm, l_hbm, *refs):
    xs, hs, ws, loss, g0, g1, gh0, gh1, gx0, gx1, pads, sems = refs
    gs = (g0, g1)
    position = lax.axis_index("section")
    parity = position & 1
    at_end = (position == 0) | (position == lax.axis_size("section") - 1)
    copies = []

    def fetch(source, target):
        copy = pltpu.make_async_copy(source, target, sems.at[len(copies)])
        copy.start()
        copies.append(copy)

    for slot in (0, 1):
        replica = parity if slot == 0 else 1 - parity
        fetch(g_hbm.at[replica], gs[slot])
        fetch(w_hbm.at[replica, 1], ws.at[slot, 1])
        fetch(h_hbm.at[replica * ticks], hs.at[slot, 0])
        fetch(w_hbm.at[replica, 0], ws.at[slot, 0])
        fetch(x_hbm.at[replica * ticks], xs.at[slot, 0])
    for slot in (0, 1):
        replica = parity if slot == 0 else 1 - parity
        later = pl.ds(replica * ticks + 1, ticks - 1)
        fetch(h_hbm.at[later], hs.at[slot, pl.ds(1, ticks - 1)])
        fetch(x_hbm.at[later], xs.at[slot, pl.ds(1, ticks - 1)])
    fetch(l_hbm.at[pl.ds((1 - parity) * (ticks - 1), ticks - 1)], loss)
    for slot, gh_ref, gx_ref in ((0, gh0, gx0), (1, gh1, gx1)):
        for copy in copies[5 * slot : 5 * slot + 5]:
            copy.wait()
        gh_ref[...], gx_ref[...] = step(
            gs[slot][...], xs.at[slot, 0], hs.at[slot, 0], ws.at[slot], pads.at[0], pads.at[1], extent
        )
    for copy in copies[10:]:
        copy.wait()

    @pl.when(jnp.logical_not(at_end))
    def _():
        loss[...] = jnp.zeros_like(loss)


def middle_kernel(extent, slot, tick, x_ref, h_ref, w_ref, g_ref, *refs):
    pads = refs[-1]
    g = g_ref[...]
    if slot == 1:
        loss_ref, gh_ref, gx_ref, used_ref = refs[:-1]
        g = (g.astype(F32) + loss_ref[tick - 1].astype(F32)).astype(BF16)
        used_ref[...] = g
    else:
        gh_ref, gx_ref = refs[:-1]
    gh_ref[...], gx_ref[...] = step(
        g,
        x_ref.at[slot, tick],
        h_ref.at[slot, tick],
        w_ref.at[slot],
        pads.at[0],
        pads.at[1],
        extent,
    )


def even_last_kernel(extent, ticks, x_ref, h_ref, w_ref, g_ref, *refs):
    early = ticks - 1
    grads_h, grads = refs[:early], refs[early : 2 * early]
    gx_ref, out_ref, pads = refs[2 * early :]
    _, gx_ref[...] = step(
        g_ref[...],
        x_ref.at[0, early],
        h_ref.at[0, early],
        w_ref.at[0],
        pads.at[1, early],
        pads.at[0, early],
        extent,
    )
    for pair, (act_ref, sides) in enumerate(((x_ref, grads_h), (h_ref, grads))):
        for n in range(early):
            fill_shifts(pads.at[pair, n], sides[n][...], extent)
        acts = [act_ref.at[0, n] for n in range(ticks)]
        total = kernel_sums(acts, [pads.at[pair, n] for n in range(ticks)], extent)
        for row, value in pieces(total, pair):
            out_ref[row : row + PIECE, :] = value.astype(BF16)


def last_kernel(extent, ticks, parts, x_ref, h_ref, w_ref, g_ref, loss_ref, gx0_ref, sums0_ref, *refs):
    early = ticks - 1
    grads_h, grads = refs[:early], refs[early : 2 * early]
    edge_ref, out_ref, pads = refs[2 * early :]
    position = lax.axis_index("section")
    parity = position & 1
    replica = 1 - parity
    g = (g_ref[...].astype(F32) + loss_ref[early - 1].astype(F32)).astype(BF16)
    _, grad_x = step(
        g,
        x_ref.at[1, early],
        h_ref.at[1, early],
        w_ref.at[1],
        pads.at[1, early],
        pads.at[0, early],
        extent,
    )
    edge_ref[replica] = grad_x
    edge_ref[parity] = gx0_ref[...]
    members, _, later, rows_each, _ = out_ref.shape
    upper = (position >= lax.axis_size("section") // 2).astype(jnp.int32)
    half0, half1 = (parity + upper) & 1, (replica + upper) & 1

    def put(row, half, value):
        shard, inner = row // rows_each, row % rows_each
        block, pair_at = shard // (2 * later), shard % (2 * later)
        member = block * (members // parts) + pair_at % 2
        out_ref[member, half, pair_at // 2, inner : inner + value.shape[0], :] = value

    for row in range(0, sums0_ref.shape[0], rows_each):
        put(row, half0, sums0_ref[row : row + rows_each, :])
    for pair, (act_ref, sides) in enumerate(((x_ref, grads_h), (h_ref, grads))):
        for n in range(early):
            fill_shifts(pads.at[pair, n], sides[n][...], extent)
        acts = [act_ref.at[1, n] for n in range(ticks)]
        total = kernel_sums(acts, [pads.at[pair, n] for n in range(ticks)], extent)
        for row, value in pieces(total, pair):
            put(row, half1, value.astype(BF16))


def call(body, steps, in_specs, out_shape, scratch, args):
    cells, channels = args[0].shape[-2:]
    return pl.pallas_call(
        body,
        in_specs=in_specs,
        out_specs=[vmem()] * len(out_shape),
        out_shape=out_shape,
        scratch_shapes=scratch,
        compiler_params=PARAMS,
        cost_estimate=pl.CostEstimate(
            flops=4 * steps * cells * TAPS * channels * channels,
            bytes_accessed=1000000,
            transcendentals=0,
        ),
    )(*args)


def vmem():
    return pl.BlockSpec(memory_space=pltpu.VMEM)


def in_hbm():
    return pl.BlockSpec(memory_space=pltpu.HBM)


def exchange(value, offset):
    total = lax.axis_size("section")
    pairs = []
    for low in range(offset, total - 1, 2):
        pairs += [(low, low + 1), (low + 1, low)]
    return lax.ppermute(value, "section", pairs)


def on_device(factors, saved_x, saved_h, kernels, grad_in, loss_grads):
    return whole(factors, saved_x, saved_h, kernels, grad_in, loss_grads)


def whole(factors, saved_x, saved_h, kernels, grad_in, loss_grads):
    ticks = saved_x.shape[1]
    extent, channels = saved_x.shape[4], saved_x.shape[6]
    cells = extent * extent
    sections = lax.axis_size("section")
    outer, inner = factors
    later, shards = inner // 2, outer * inner
    rows = 2 * TAPS * channels
    field = (cells, channels)

    def shape(*lead, tail=field):
        return jax.ShapeDtypeStruct((*lead, *tail), BF16)

    def pads(*lead):
        return pltpu.VMEM((*lead, 3, cells + 2 * extent, channels), BF16)

    xs, hs, ws, loss, g0, g1, gh0, gh1, out0, out1 = call(
        functools.partial(first_kernel, extent, ticks),
        2,
        [in_hbm()] * 5,
        [
            shape(2, ticks),
            shape(2, ticks),
            shape(*kernels.shape[1:-2], tail=(channels, channels)),
            shape(ticks - 1),
            *[shape()] * 6,
        ],
        [pads(2), pltpu.SemaphoreType.DMA((15,))],
        [
            pltpu.with_memory_space_constraint(value, pltpu.HBM)
            for value in (
                saved_x.reshape(-1, *field),
                saved_h.reshape(-1, *field),
                kernels[0],
                grad_in.reshape(-1, *field),
                loss_grads.reshape(-1, *field),
            )
        ],
    )
    g, gh = [[g0], [g1]], [[gh0], [gh1]]
    for tick in range(1, ticks):
        far = exchange(out0, 1)
        near = exchange(out1, 0)
        if tick == ticks - 1:
            break
        gh0, out0 = call(
            functools.partial(middle_kernel, extent, 0, tick),
            1,
            [vmem()] * 4,
            [shape(), shape()],
            [pads(2)],
            (xs, hs, ws, near),
        )
        gh1, out1, g1 = call(
            functools.partial(middle_kernel, extent, 1, tick),
            1,
            [vmem()] * 5,
            [shape(), shape(), shape()],
            [pads(2)],
            (xs, hs, ws, far, loss),
        )
        for slot, used, made in ((0, near, gh0), (1, g1, gh1)):
            g[slot].append(used)
            gh[slot].append(made)
    out0, sums0 = call(
        functools.partial(even_last_kernel, extent, ticks),
        1 + ticks,
        [vmem()] * (4 + 2 * (ticks - 1)),
        [shape(), shape(tail=(rows, channels))],
        [pads(2, ticks)],
        (xs, hs, ws, near, *gh[0], *g[0]),
    )
    edge, both = call(
        functools.partial(last_kernel, extent, ticks, outer),
        1 + ticks,
        [vmem()] * (7 + 2 * (ticks - 1)),
        [shape(2), shape(2 * outer, 2, later, rows // shards, tail=(channels,))],
        [pads(2, ticks)],
        (xs, hs, ws, far, loss, out0, sums0, *gh[1], *g[1]),
    )
    edge_grads = edge.reshape(2, 1, 1, extent, extent, channels)

    def shard(block, far, near):
        return (block * later + far) * 2 + near

    first_groups = [
        [shard(block, far, near) for block in range(outer) for near in range(2)]
        for far in range(later)
    ]
    second_groups = [
        [
            section * shards + shard(block, far, near)
            for section in (low, sections - 1 - low)
            for far in range(later)
        ]
        for low in range(sections // 2)
        for block in range(outer)
        for near in range(2)
    ]

    def total(value):
        parts = [value[n].astype(F32) for n in range(value.shape[0])]
        return functools.reduce(lambda a, b: a + b, parts)

    both = lax.all_to_all(both, "dp", 0, 0, axis_index_groups=first_groups, tiled=True)
    both = total(both).astype(BF16).reshape(2 * later, rows // shards, channels)
    both = lax.all_to_all(
        both, ("section", "dp"), 0, 0, axis_index_groups=second_groups, tiled=True
    )
    kernel_grads = (total(both) * (1.0 / float(cells)))[None]
    return (kernel_grads, edge_grads)


def solution(mesh):
    shards = mesh.shape["dp"]
    outer = next(f for f in (4, 2, 1) if shards % f == 0)
    return jax.shard_map(
        functools.partial(on_device, (outer, shards // outer)),
        mesh=mesh,
        in_specs=(
            P(None, None, "section", "dp", None, None, None),
            P(None, None, "section", "dp", None, None, None),
            P("section", None, None, None, None, None),
            P(None, "section", "dp", None, None, None),
            P(None, None, "dp", None, None, None),
        ),
        out_specs=(P("section", "dp", None), P(None, "section", "dp", None, None, None)),
        check_vma=False,
    )
```

```python
import functools

import jax
import jax.numpy as jnp
from jax import lax
from jax.experimental import pallas as pl
from jax.experimental.pallas import tpu as pltpu
from jax.sharding import PartitionSpec as P


TAPS = 9
PIECE = 16
PARAMS = pltpu.CompilerParams(vmem_limit_bytes=16 << 20)
BF16, F32 = jnp.bfloat16, jnp.float32


def moved_along_x(value, extent):
    cells, channels = value.shape
    wide = value.astype(F32)
    column = lax.broadcasted_iota(jnp.int32, (cells, channels), 0) & (extent - 1)
    left = jnp.where(column == extent - 1, 0.0, pltpu.roll(wide, cells - 1, 0))
    right = jnp.where(column == 0, 0.0, pltpu.roll(wide, 1, 0))
    return jnp.concatenate([left.astype(value.dtype), value, right.astype(value.dtype)], axis=1)


def down(value, extent):
    return jnp.concatenate([jnp.zeros_like(value[:extent]), value[:-extent]], axis=0)


def up(value, extent):
    return jnp.concatenate([value[extent:], jnp.zeros_like(value[:extent])], axis=0)


def conv_back(moved, w_ref, extent):
    rows = [jnp.concatenate([w_ref[3 * r + c] for c in range(3)], axis=1) for r in range(3)]
    result = lax.dot_general(
        moved,
        jnp.concatenate(rows, axis=0),
        (((1,), (1,)), ((), ())),
        preferred_element_type=F32,
    )
    above, level, below = jnp.split(result, 3, axis=1)
    return level + down(below, extent) + up(above, extent)


def step(g, x_ref, h_ref, w_ref, mg_ref, mh_ref, extent, between=None):
    mg_ref[...] = moved_along_x(g, extent)
    grad_z = conv_back(mg_ref[...], w_ref.at[1], extent)
    grad_h = jnp.where(h_ref[...].astype(F32) > 0, grad_z, 0.0).astype(BF16)
    mh_ref[...] = moved_along_x(grad_h, extent)
    if between is not None:
        between()
    grad_u = conv_back(mh_ref[...], w_ref.at[0], extent)
    passed = jnp.where(x_ref[...].astype(F32) > 0, grad_u, 0.0)
    return (g.astype(F32) + passed).astype(BF16)


def kernel_sums(act_refs, moved_refs, extent):
    rows = []
    for act_ref in act_refs:
        act = jnp.maximum(act_ref[...].astype(F32), 0.0).astype(BF16)
        rows.append(jnp.concatenate([down(act, extent), act, up(act, extent)], axis=1))
    return lax.dot_general(
        jnp.concatenate(rows, axis=0),
        jnp.concatenate([moved[...] for moved in moved_refs], axis=0),
        (((0,), (0,)), ((), ())),
        preferred_element_type=F32,
    )


def pieces(total, pair):
    channels = total.shape[0] // 3
    for k in range(TAPS):
        for start in range(0, channels, PIECE):
            top, left = k // 3 * channels + start, k % 3 * channels
            values = total[top : top + PIECE, left : left + channels]
            yield (pair * TAPS + k) * channels + start, values


def first_kernel(extent, ticks, x_hbm, h_hbm, w_hbm, g_hbm, l_hbm, *refs):
    xs, hs, ws, loss, mg0, mg1, mh0, mh1, gx0, gx1, gs, sems = refs
    position = lax.axis_index("section")
    parity = position & 1
    at_end = (position == 0) | (position == lax.axis_size("section") - 1)
    copies = []

    def fetch(source, target):
        copy = pltpu.make_async_copy(source, target, sems.at[len(copies)])
        copy.start()
        copies.append(copy)

    for slot in (0, 1):
        replica = parity if slot == 0 else 1 - parity
        fetch(g_hbm.at[replica], gs.at[slot])
        fetch(w_hbm.at[replica, 1], ws.at[slot, 1])
        fetch(h_hbm.at[replica * ticks], hs.at[slot, 0])
        fetch(w_hbm.at[replica, 0], ws.at[slot, 0])
        fetch(x_hbm.at[replica * ticks], xs.at[slot, 0])
    for slot in (0, 1):
        replica = parity if slot == 0 else 1 - parity
        later = pl.ds(replica * ticks + 1, ticks - 1)
        fetch(h_hbm.at[later], hs.at[slot, pl.ds(1, ticks - 1)])
        fetch(x_hbm.at[later], xs.at[slot, pl.ds(1, ticks - 1)])
    fetch(l_hbm.at[pl.ds((1 - parity) * (ticks - 1), ticks - 1)], loss)
    for slot, mg_ref, mh_ref, gx_ref in ((0, mg0, mh0, gx0), (1, mg1, mh1, gx1)):
        needed = copies[5 * slot : 5 * slot + 5]

        def wait(some):
            for copy in some:
                copy.wait()

        wait(needed[:3])
        gx_ref[...] = step(
            gs[slot],
            xs.at[slot, 0],
            hs.at[slot, 0],
            ws.at[slot],
            mg_ref,
            mh_ref,
            extent,
            functools.partial(wait, needed[3:]),
        )
    for copy in copies[10:]:
        copy.wait()

    @pl.when(jnp.logical_not(at_end))
    def _():
        loss[...] = jnp.zeros_like(loss)


def middle_kernel(extent, slot, tick, x_ref, h_ref, w_ref, g_ref, *refs):
    g = g_ref[...]
    if slot == 1:
        g = (g.astype(F32) + refs[0][tick - 1].astype(F32)).astype(BF16)
    mg_ref, mh_ref, gx_ref = refs[-3:]
    gx_ref[...] = step(
        g, x_ref.at[slot, tick], h_ref.at[slot, tick], w_ref.at[slot], mg_ref, mh_ref, extent
    )


def even_last_kernel(extent, ticks, x_ref, h_ref, w_ref, g_ref, *refs):
    early = ticks - 1
    moved_h, moved_g = refs[:early], refs[early : 2 * early]
    gx_ref, out_ref, mg_ref, mh_ref = refs[2 * early :]
    gx_ref[...] = step(
        g_ref[...],
        x_ref.at[0, early],
        h_ref.at[0, early],
        w_ref.at[0],
        mg_ref,
        mh_ref,
        extent,
    )
    for pair, act_ref, moved in ((0, x_ref, (*moved_h, mh_ref)), (1, h_ref, (*moved_g, mg_ref))):
        total = kernel_sums([act_ref.at[0, n] for n in range(ticks)], moved, extent)
        for row, value in pieces(total, pair):
            out_ref[row : row + PIECE, :] = value.astype(BF16)


def last_kernel(extent, ticks, parts, x_ref, h_ref, w_ref, g_ref, loss_ref, gx0_ref, sums0_ref, *refs):
    early = ticks - 1
    moved_h, moved_g = refs[:early], refs[early : 2 * early]
    edge_hbm, out_ref, mg_ref, mh_ref, gx1_ref, sems = refs[2 * early :]
    position = lax.axis_index("section")
    parity = position & 1
    g = (g_ref[...].astype(F32) + loss_ref[early - 1].astype(F32)).astype(BF16)
    copies = [
        pltpu.make_async_copy(gx0_ref, edge_hbm.at[parity], sems.at[0]),
        pltpu.make_async_copy(gx1_ref, edge_hbm.at[1 - parity], sems.at[1]),
    ]
    copies[0].start()
    gx1_ref[...] = step(
        g, x_ref.at[1, early], h_ref.at[1, early], w_ref.at[1], mg_ref, mh_ref, extent
    )
    members, _, later, rows_each, _ = out_ref.shape
    upper = (position >= lax.axis_size("section") // 2).astype(jnp.int32)
    half0, half1 = (parity + upper) & 1, (1 - parity + upper) & 1

    def put(row, half, value):
        shard, inner = row // rows_each, row % rows_each
        block, pair_at = shard // (2 * later), shard % (2 * later)
        member = block * (members // parts) + pair_at % 2
        out_ref[member, half, pair_at // 2, inner : inner + value.shape[0], :] = value

    for row in range(0, sums0_ref.shape[0], rows_each):
        put(row, half0, sums0_ref[row : row + rows_each, :])
    copies[1].start()
    for pair, act_ref, moved in ((0, x_ref, (*moved_h, mh_ref)), (1, h_ref, (*moved_g, mg_ref))):
        total = kernel_sums([act_ref.at[1, n] for n in range(ticks)], moved, extent)
        for row, value in pieces(total, pair):
            put(row, half1, value.astype(BF16))
    for copy in copies:
        copy.wait()


def call(body, steps, in_specs, out_shape, scratch, args, hbm_outs=0):
    cells, channels = args[0].shape[-2:]
    return pl.pallas_call(
        body,
        in_specs=in_specs,
        out_specs=[in_hbm()] * hbm_outs + [vmem()] * (len(out_shape) - hbm_outs),
        out_shape=out_shape,
        scratch_shapes=scratch,
        compiler_params=PARAMS,
        cost_estimate=pl.CostEstimate(
            flops=4 * steps * cells * TAPS * channels * channels,
            bytes_accessed=1000000,
            transcendentals=0,
        ),
    )(*args)


def vmem():
    return pl.BlockSpec(memory_space=pltpu.VMEM)


def in_hbm():
    return pl.BlockSpec(memory_space=pltpu.HBM)


def exchange(value, offset):
    total = lax.axis_size("section")
    pairs = []
    for low in range(offset, total - 1, 2):
        pairs += [(low, low + 1), (low + 1, low)]
    return lax.ppermute(value, "section", pairs)


def on_device(factors, saved_x, saved_h, kernels, grad_in, loss_grads):
    return whole(factors, saved_x, saved_h, kernels, grad_in, loss_grads)


def whole(factors, saved_x, saved_h, kernels, grad_in, loss_grads):
    ticks = saved_x.shape[1]
    extent, channels = saved_x.shape[4], saved_x.shape[6]
    cells = extent * extent
    sections = lax.axis_size("section")
    outer, inner = factors
    later, shards = inner // 2, outer * inner
    rows = 2 * TAPS * channels
    field = (cells, channels)

    def shape(*lead, tail=field):
        return jax.ShapeDtypeStruct((*lead, *tail), BF16)

    moved = shape(tail=(cells, 3 * channels))
    scratch = [pltpu.VMEM(moved.shape, BF16)] * 2

    xs, hs, ws, loss, mg0, mg1, mh0, mh1, out0, out1 = call(
        functools.partial(first_kernel, extent, ticks),
        2,
        [in_hbm()] * 5,
        [
            shape(2, ticks),
            shape(2, ticks),
            shape(*kernels.shape[1:-2], tail=(channels, channels)),
            shape(ticks - 1),
            *[moved] * 4,
            *[shape()] * 2,
        ],
        [pltpu.VMEM((2, *field), BF16), pltpu.SemaphoreType.DMA((15,))],
        [
            pltpu.with_memory_space_constraint(value, pltpu.HBM)
            for value in (
                saved_x.reshape(-1, *field),
                saved_h.reshape(-1, *field),
                kernels[0],
                grad_in.reshape(-1, *field),
                loss_grads.reshape(-1, *field),
            )
        ],
    )
    mg, mh = [[mg0], [mg1]], [[mh0], [mh1]]
    for tick in range(1, ticks):
        far = exchange(out0, 1)
        near = exchange(out1, 0)
        if tick == ticks - 1:
            break
        mg0, mh0, out0 = call(
            functools.partial(middle_kernel, extent, 0, tick),
            1,
            [vmem()] * 4,
            [moved, moved, shape()],
            [],
            (xs, hs, ws, near),
        )
        mg1, mh1, out1 = call(
            functools.partial(middle_kernel, extent, 1, tick),
            1,
            [vmem()] * 5,
            [moved, moved, shape()],
            [],
            (xs, hs, ws, far, loss),
        )
        for slot, used, made in ((0, mg0, mh0), (1, mg1, mh1)):
            mg[slot].append(used)
            mh[slot].append(made)
    out0, sums0 = call(
        functools.partial(even_last_kernel, extent, ticks),
        1 + ticks,
        [vmem()] * (4 + 2 * (ticks - 1)),
        [shape(), shape(tail=(rows, channels))],
        scratch,
        (xs, hs, ws, near, *mh[0], *mg[0]),
    )
    edge, both = call(
        functools.partial(last_kernel, extent, ticks, outer),
        1 + ticks,
        [vmem()] * (7 + 2 * (ticks - 1)),
        [shape(2), shape(2 * outer, 2, later, rows // shards, tail=(channels,))],
        [*scratch, pltpu.VMEM(field, BF16), pltpu.SemaphoreType.DMA((2,))],
        (xs, hs, ws, far, loss, out0, sums0, *mh[1], *mg[1]),
        hbm_outs=1,
    )
    edge_grads = edge.reshape(2, 1, 1, extent, extent, channels)

    def shard(block, far, near):
        return (block * later + far) * 2 + near

    first_groups = [
        [shard(block, far, near) for block in range(outer) for near in range(2)]
        for far in range(later)
    ]
    second_groups = [
        [
            section * shards + shard(block, far, near)
            for section in (low, sections - 1 - low)
            for far in range(later)
        ]
        for low in range(sections // 2)
        for block in range(outer)
        for near in range(2)
    ]

    def total(value):
        parts = [value[n].astype(F32) for n in range(value.shape[0])]
        return functools.reduce(lambda a, b: a + b, parts)

    both = lax.all_to_all(both, "dp", 0, 0, axis_index_groups=first_groups, tiled=True)
    both = total(both).astype(BF16).reshape(2 * later, rows // shards, channels)
    both = lax.all_to_all(
        both, ("section", "dp"), 0, 0, axis_index_groups=second_groups, tiled=True
    )
    kernel_grads = (total(both) * (1.0 / float(cells)))[None]
    return (kernel_grads, edge_grads)


def solution(mesh):
    shards = mesh.shape["dp"]
    outer = next(f for f in (4, 2, 1) if shards % f == 0)
    return jax.shard_map(
        functools.partial(on_device, (outer, shards // outer)),
        mesh=mesh,
        in_specs=(
            P(None, None, "section", "dp", None, None, None),
            P(None, None, "section", "dp", None, None, None),
            P("section", None, None, None, None, None),
            P(None, "section", "dp", None, None, None),
            P(None, None, "dp", None, None, None),
        ),
        out_specs=(P("section", "dp", None), P(None, "section", "dp", None, None, None)),
        check_vma=False,
    )
```

```python
import functools

import jax
import jax.numpy as jnp
from jax import lax
from jax.experimental import pallas as pl
from jax.experimental.pallas import tpu as pltpu
from jax.sharding import PartitionSpec as P


TAPS = 9
PIECE = 16
PARAMS = pltpu.CompilerParams(vmem_limit_bytes=16 << 20)
BF16, F32 = jnp.bfloat16, jnp.float32


def moved_along_x(value, extent):
    cells, channels = value.shape
    wide = value.astype(F32)
    column = lax.broadcasted_iota(jnp.int32, (cells, channels), 0) & (extent - 1)
    left = jnp.where(column == extent - 1, 0.0, pltpu.roll(wide, cells - 1, 0))
    right = jnp.where(column == 0, 0.0, pltpu.roll(wide, 1, 0))
    return jnp.concatenate([left.astype(value.dtype), value, right.astype(value.dtype)], axis=1)


def down(value, extent):
    return jnp.concatenate([jnp.zeros_like(value[:extent]), value[:-extent]], axis=0)


def up(value, extent):
    return jnp.concatenate([value[extent:], jnp.zeros_like(value[:extent])], axis=0)


def conv_back(moved, w_ref, extent):
    rows = [jnp.concatenate([w_ref[3 * r + c] for c in range(3)], axis=1) for r in range(3)]
    result = lax.dot_general(
        moved,
        jnp.concatenate(rows, axis=0),
        (((1,), (1,)), ((), ())),
        preferred_element_type=F32,
    )
    above, level, below = jnp.split(result, 3, axis=1)
    return level + down(below, extent) + up(above, extent)


def step(g, x_ref, h_ref, w_ref, mg_ref, mh_ref, extent, between=None):
    mg_ref[...] = moved_along_x(g, extent)
    grad_z = conv_back(mg_ref[...], w_ref.at[1], extent)
    grad_h = jnp.where(h_ref[...].astype(F32) > 0, grad_z, 0.0).astype(BF16)
    mh_ref[...] = moved_along_x(grad_h, extent)
    if between is not None:
        between()
    grad_u = conv_back(mh_ref[...], w_ref.at[0], extent)
    passed = jnp.where(x_ref[...].astype(F32) > 0, grad_u, 0.0)
    return (g.astype(F32) + passed).astype(BF16)


def kernel_sums(act_refs, moved_refs, extent):
    rows = []
    for act_ref in act_refs:
        act = jnp.maximum(act_ref[...].astype(F32), 0.0).astype(BF16)
        rows.append(jnp.concatenate([down(act, extent), act, up(act, extent)], axis=1))
    return lax.dot_general(
        jnp.concatenate(rows, axis=0),
        jnp.concatenate([moved[...] for moved in moved_refs], axis=0),
        (((0,), (0,)), ((), ())),
        preferred_element_type=F32,
    )


def pieces(total, pair):
    channels = total.shape[0] // 3
    for k in range(TAPS):
        for start in range(0, channels, PIECE):
            top, left = k // 3 * channels + start, k % 3 * channels
            values = total[top : top + PIECE, left : left + channels]
            yield (pair * TAPS + k) * channels + start, values


def first_kernel(extent, ticks, x_hbm, h_hbm, w_hbm, g_hbm, l_hbm, *refs):
    xs, hs, ws, loss, mg0, mg1, mh0, mh1, gx0, gx1, gs, sems = refs
    position = lax.axis_index("section")
    parity = position & 1
    at_end = (position == 0) | (position == lax.axis_size("section") - 1)
    copies = []

    def fetch(source, target):
        copy = pltpu.make_async_copy(source, target, sems.at[len(copies)])
        copy.start()
        copies.append(copy)

    def fetch_first(slot):
        replica = parity if slot == 0 else 1 - parity
        fetch(g_hbm.at[replica], gs.at[slot])
        fetch(w_hbm.at[replica, 1], ws.at[slot, 1])
        fetch(h_hbm.at[replica * ticks], hs.at[slot, 0])
        fetch(w_hbm.at[replica, 0], ws.at[slot, 0])
        fetch(x_hbm.at[replica * ticks], xs.at[slot, 0])

    def fetch_later():
        for slot in (0, 1):
            replica = parity if slot == 0 else 1 - parity
            later = pl.ds(replica * ticks + 1, ticks - 1)
            fetch(h_hbm.at[later], hs.at[slot, pl.ds(1, ticks - 1)])
            fetch(x_hbm.at[later], xs.at[slot, pl.ds(1, ticks - 1)])
        fetch(l_hbm.at[pl.ds((1 - parity) * (ticks - 1), ticks - 1)], loss)

    def wait(first, last):
        for copy in copies[first:last]:
            copy.wait()

    fetch_first(0)
    wait(0, 3)
    fetch_first(1)

    def middle_of_slot_0():
        wait(3, 5)
        fetch_later()

    gx0[...] = step(
        gs[0], xs.at[0, 0], hs.at[0, 0], ws.at[0], mg0, mh0, extent, middle_of_slot_0
    )
    wait(5, 8)
    gx1[...] = step(
        gs[1], xs.at[1, 0], hs.at[1, 0], ws.at[1], mg1, mh1, extent, lambda: wait(8, 10)
    )
    wait(10, len(copies))

    @pl.when(jnp.logical_not(at_end))
    def _():
        loss[...] = jnp.zeros_like(loss)


def middle_kernel(extent, slot, tick, x_ref, h_ref, w_ref, g_ref, *refs):
    g = g_ref[...]
    if slot == 1:
        g = (g.astype(F32) + refs[0][tick - 1].astype(F32)).astype(BF16)
    mg_ref, mh_ref, gx_ref = refs[-3:]
    gx_ref[...] = step(
        g, x_ref.at[slot, tick], h_ref.at[slot, tick], w_ref.at[slot], mg_ref, mh_ref, extent
    )


def early_kernel(extent, early, x_ref, h_ref, *refs):
    out_refs = refs[-2:]
    for slot in (0, 1):
        mine = refs[2 * early * slot : 2 * early * (slot + 1)]
        for pair, act_ref, moved in ((0, x_ref, mine[:early]), (1, h_ref, mine[early:])):
            total = kernel_sums([act_ref.at[slot, n] for n in range(early)], moved, extent)
            for row, value in pieces(total, pair):
                out_refs[slot][row : row + PIECE, :] = value


def even_last_kernel(extent, early, x_ref, h_ref, w_ref, g_ref, acc_ref, *refs):
    gx_ref, out_ref, mg_ref, mh_ref = refs
    gx_ref[...] = step(
        g_ref[...],
        x_ref.at[0, early],
        h_ref.at[0, early],
        w_ref.at[0],
        mg_ref,
        mh_ref,
        extent,
    )
    for pair, act_ref, moved_ref in ((0, x_ref, mh_ref), (1, h_ref, mg_ref)):
        total = kernel_sums([act_ref.at[0, early]], [moved_ref], extent)
        for row, value in pieces(total, pair):
            value = value + acc_ref[row : row + PIECE, :]
            out_ref[row : row + PIECE, :] = value.astype(BF16)


def last_kernel(extent, early, parts, x_ref, h_ref, w_ref, g_ref, loss_ref, *refs):
    gx0_ref, sums0_ref, acc_ref, edge_hbm, out_ref, mg_ref, mh_ref, gx1_ref, sems = refs
    position = lax.axis_index("section")
    parity = position & 1
    g = (g_ref[...].astype(F32) + loss_ref[early - 1].astype(F32)).astype(BF16)
    copies = [
        pltpu.make_async_copy(gx0_ref, edge_hbm.at[parity], sems.at[0]),
        pltpu.make_async_copy(gx1_ref, edge_hbm.at[1 - parity], sems.at[1]),
    ]
    copies[0].start()
    gx1_ref[...] = step(
        g, x_ref.at[1, early], h_ref.at[1, early], w_ref.at[1], mg_ref, mh_ref, extent
    )
    members, _, later, rows_each, _ = out_ref.shape
    upper = (position >= lax.axis_size("section") // 2).astype(jnp.int32)
    half0, half1 = (parity + upper) & 1, (1 - parity + upper) & 1

    def put(row, half, value):
        shard, inner = row // rows_each, row % rows_each
        block, pair_at = shard // (2 * later), shard % (2 * later)
        member = block * (members // parts) + pair_at % 2
        out_ref[member, half, pair_at // 2, inner : inner + value.shape[0], :] = value

    for row in range(0, sums0_ref.shape[0], rows_each):
        put(row, half0, sums0_ref[row : row + rows_each, :])
    copies[1].start()
    for pair, act_ref, moved_ref in ((0, x_ref, mh_ref), (1, h_ref, mg_ref)):
        total = kernel_sums([act_ref.at[1, early]], [moved_ref], extent)
        for row, value in pieces(total, pair):
            put(row, half1, (value + acc_ref[row : row + PIECE, :]).astype(BF16))
    for copy in copies:
        copy.wait()


def call(body, steps, in_specs, out_shape, scratch, args, hbm_outs=0):
    cells, channels = args[0].shape[-2:]
    return pl.pallas_call(
        body,
        in_specs=in_specs,
        out_specs=[in_hbm()] * hbm_outs + [vmem()] * (len(out_shape) - hbm_outs),
        out_shape=out_shape,
        scratch_shapes=scratch,
        compiler_params=PARAMS,
        cost_estimate=pl.CostEstimate(
            flops=4 * steps * cells * TAPS * channels * channels,
            bytes_accessed=1000000,
            transcendentals=0,
        ),
    )(*args)


def vmem():
    return pl.BlockSpec(memory_space=pltpu.VMEM)


def in_hbm():
    return pl.BlockSpec(memory_space=pltpu.HBM)


def exchange(value, offset):
    total = lax.axis_size("section")
    pairs = []
    for low in range(offset, total - 1, 2):
        pairs += [(low, low + 1), (low + 1, low)]
    return lax.ppermute(value, "section", pairs)


def on_device(factors, saved_x, saved_h, kernels, grad_in, loss_grads):
    return whole(factors, saved_x, saved_h, kernels, grad_in, loss_grads)


def whole(factors, saved_x, saved_h, kernels, grad_in, loss_grads):
    ticks = saved_x.shape[1]
    extent, channels = saved_x.shape[4], saved_x.shape[6]
    cells = extent * extent
    sections = lax.axis_size("section")
    outer, inner = factors
    later, shards = inner // 2, outer * inner
    rows = 2 * TAPS * channels
    field = (cells, channels)

    def shape(*lead, tail=field):
        return jax.ShapeDtypeStruct((*lead, *tail), BF16)

    moved = shape(tail=(cells, 3 * channels))
    scratch = [pltpu.VMEM(moved.shape, BF16)] * 2

    xs, hs, ws, loss, mg0, mg1, mh0, mh1, out0, out1 = call(
        functools.partial(first_kernel, extent, ticks),
        2,
        [in_hbm()] * 5,
        [
            shape(2, ticks),
            shape(2, ticks),
            shape(*kernels.shape[1:-2], tail=(channels, channels)),
            shape(ticks - 1),
            *[moved] * 4,
            *[shape()] * 2,
        ],
        [pltpu.VMEM((2, *field), BF16), pltpu.SemaphoreType.DMA((15,))],
        [
            pltpu.with_memory_space_constraint(value, pltpu.HBM)
            for value in (
                saved_x.reshape(-1, *field),
                saved_h.reshape(-1, *field),
                kernels[0],
                grad_in.reshape(-1, *field),
                loss_grads.reshape(-1, *field),
            )
        ],
    )
    mg, mh = [[mg0], [mg1]], [[mh0], [mh1]]
    for tick in range(1, ticks):
        far = exchange(out0, 1)
        near = exchange(out1, 0)
        if tick == ticks - 1:
            break
        mg0, mh0, out0 = call(
            functools.partial(middle_kernel, extent, 0, tick),
            1,
            [vmem()] * 4,
            [moved, moved, shape()],
            [],
            (xs, hs, ws, near),
        )
        mg1, mh1, out1 = call(
            functools.partial(middle_kernel, extent, 1, tick),
            1,
            [vmem()] * 5,
            [moved, moved, shape()],
            [],
            (xs, hs, ws, far, loss),
        )
        for slot, used, made in ((0, mg0, mh0), (1, mg1, mh1)):
            mg[slot].append(used)
            mh[slot].append(made)
    early = ticks - 1
    sums = jax.ShapeDtypeStruct((rows, channels), F32)
    acc0, acc1 = call(
        functools.partial(early_kernel, extent, early),
        2 * early,
        [vmem()] * (2 + 4 * early),
        [sums, sums],
        [],
        (xs, hs, *mh[0], *mg[0], *mh[1], *mg[1]),
    )
    out0, sums0 = call(
        functools.partial(even_last_kernel, extent, early),
        2,
        [vmem()] * 5,
        [shape(), shape(tail=(rows, channels))],
        scratch,
        (xs, hs, ws, near, acc0),
    )
    edge, both = call(
        functools.partial(last_kernel, extent, early, outer),
        2,
        [vmem()] * 8,
        [shape(2), shape(2 * outer, 2, later, rows // shards, tail=(channels,))],
        [*scratch, pltpu.VMEM(field, BF16), pltpu.SemaphoreType.DMA((2,))],
        (xs, hs, ws, far, loss, out0, sums0, acc1),
        hbm_outs=1,
    )
    edge_grads = edge.reshape(2, 1, 1, extent, extent, channels)

    def shard(block, far, near):
        return (block * later + far) * 2 + near

    first_groups = [
        [shard(block, far, near) for block in range(outer) for near in range(2)]
        for far in range(later)
    ]
    second_groups = [
        [
            section * shards + shard(block, far, near)
            for section in (low, sections - 1 - low)
            for far in range(later)
        ]
        for low in range(sections // 2)
        for block in range(outer)
        for near in range(2)
    ]

    def total(value):
        parts = [value[n].astype(F32) for n in range(value.shape[0])]
        return functools.reduce(lambda a, b: a + b, parts)

    both = lax.all_to_all(both, "dp", 0, 0, axis_index_groups=first_groups, tiled=True)
    both = total(both).astype(BF16).reshape(2 * later, rows // shards, channels)
    both = lax.all_to_all(
        both, ("section", "dp"), 0, 0, axis_index_groups=second_groups, tiled=True
    )
    kernel_grads = (total(both) * (1.0 / float(cells)))[None]
    return (kernel_grads, edge_grads)


def solution(mesh):
    shards = mesh.shape["dp"]
    outer = next(f for f in (4, 2, 1) if shards % f == 0)
    return jax.shard_map(
        functools.partial(on_device, (outer, shards // outer)),
        mesh=mesh,
        in_specs=(
            P(None, None, "section", "dp", None, None, None),
            P(None, None, "section", "dp", None, None, None),
            P("section", None, None, None, None, None),
            P(None, "section", "dp", None, None, None),
            P(None, None, "dp", None, None, None),
        ),
        out_specs=(P("section", "dp", None), P(None, "section", "dp", None, None, None)),
        check_vma=False,
    )
```

```python
import functools

import jax
import jax.numpy as jnp
from jax import lax
from jax.experimental import pallas as pl
from jax.experimental.pallas import tpu as pltpu
from jax.sharding import PartitionSpec as P


TAPS = 9
PIECE = 16
PARAMS = pltpu.CompilerParams(vmem_limit_bytes=16 << 20)
BF16, F32 = jnp.bfloat16, jnp.float32


def moved_along_x(value, extent):
    cells, channels = value.shape
    wide = value.astype(F32)
    column = lax.broadcasted_iota(jnp.int32, (cells, channels), 0) & (extent - 1)
    left = jnp.where(column == extent - 1, 0.0, pltpu.roll(wide, cells - 1, 0))
    right = jnp.where(column == 0, 0.0, pltpu.roll(wide, 1, 0))
    return jnp.concatenate([left.astype(value.dtype), value, right.astype(value.dtype)], axis=1)


def down(value, extent):
    return jnp.concatenate([jnp.zeros_like(value[:extent]), value[:-extent]], axis=0)


def up(value, extent):
    return jnp.concatenate([value[extent:], jnp.zeros_like(value[:extent])], axis=0)


def conv_back(moved, w_ref, extent):
    rows = [jnp.concatenate([w_ref[3 * r + c] for c in range(3)], axis=1) for r in range(3)]
    result = lax.dot_general(
        moved,
        jnp.concatenate(rows, axis=0),
        (((1,), (1,)), ((), ())),
        preferred_element_type=F32,
    )
    above, level, below = jnp.split(result, 3, axis=1)
    return level + down(below, extent) + up(above, extent)


def step(g, x_ref, h_ref, w_ref, mg_ref, mh_ref, extent, between=None):
    mg_ref[...] = moved_along_x(g, extent)
    grad_z = conv_back(mg_ref[...], w_ref.at[1], extent)
    grad_h = jnp.where(h_ref[...].astype(F32) > 0, grad_z, 0.0).astype(BF16)
    mh_ref[...] = moved_along_x(grad_h, extent)
    if between is not None:
        between()
    grad_u = conv_back(mh_ref[...], w_ref.at[0], extent)
    passed = jnp.where(x_ref[...].astype(F32) > 0, grad_u, 0.0)
    return (g.astype(F32) + passed).astype(BF16)


def kernel_sums(act_refs, moved_refs, extent):
    rows = []
    for act_ref in act_refs:
        act = jnp.maximum(act_ref[...].astype(F32), 0.0).astype(BF16)
        rows.append(jnp.concatenate([down(act, extent), act, up(act, extent)], axis=1))
    return lax.dot_general(
        jnp.concatenate(rows, axis=0),
        jnp.concatenate([moved[...] for moved in moved_refs], axis=0),
        (((0,), (0,)), ((), ())),
        preferred_element_type=F32,
    )


def pieces(total, pair):
    channels = total.shape[0] // 3
    for k in range(TAPS):
        for start in range(0, channels, PIECE):
            top, left = k // 3 * channels + start, k % 3 * channels
            values = total[top : top + PIECE, left : left + channels]
            yield (pair * TAPS + k) * channels + start, values


def first_kernel(extent, ticks, x_hbm, h_hbm, w_hbm, g_hbm, l_hbm, *refs):
    xs, hs, ws, loss, mg0, mg1, mh0, mh1, gx0, gx1, gs, sems = refs
    position = lax.axis_index("section")
    parity = position & 1
    at_end = (position == 0) | (position == lax.axis_size("section") - 1)
    copies = []

    def fetch(source, target):
        copy = pltpu.make_async_copy(source, target, sems.at[len(copies)])
        copy.start()
        copies.append(copy)

    for slot in (0, 1):
        replica = parity if slot == 0 else 1 - parity
        fetch(g_hbm.at[replica], gs.at[slot])
        fetch(w_hbm.at[replica, 1], ws.at[slot, 1])
        fetch(h_hbm.at[replica * ticks], hs.at[slot, 0])
        fetch(w_hbm.at[replica, 0], ws.at[slot, 0])
        fetch(x_hbm.at[replica * ticks], xs.at[slot, 0])
    for slot in (0, 1):
        replica = parity if slot == 0 else 1 - parity
        later = pl.ds(replica * ticks + 1, ticks - 1)
        fetch(h_hbm.at[later], hs.at[slot, pl.ds(1, ticks - 1)])
        fetch(x_hbm.at[later], xs.at[slot, pl.ds(1, ticks - 1)])
    fetch(l_hbm.at[pl.ds((1 - parity) * (ticks - 1), ticks - 1)], loss)

    def wait(first, last):
        for copy in copies[first:last]:
            copy.wait()

    wait(0, 3)
    gx0[...] = step(
        gs[0], xs.at[0, 0], hs.at[0, 0], ws.at[0], mg0, mh0, extent, lambda: wait(3, 5)
    )
    wait(5, 8)
    gx1[...] = step(
        gs[1], xs.at[1, 0], hs.at[1, 0], ws.at[1], mg1, mh1, extent, lambda: wait(8, 10)
    )
    wait(10, len(copies))

    @pl.when(jnp.logical_not(at_end))
    def _():
        loss[...] = jnp.zeros_like(loss)


def middle_kernel(extent, slot, tick, x_ref, h_ref, w_ref, g_ref, *refs):
    g = g_ref[...]
    if slot == 1:
        g = (g.astype(F32) + refs[0][tick - 1].astype(F32)).astype(BF16)
    mg_ref, mh_ref, gx_ref = refs[-3:]
    gx_ref[...] = step(
        g, x_ref.at[slot, tick], h_ref.at[slot, tick], w_ref.at[slot], mg_ref, mh_ref, extent
    )


def early_kernel(extent, early, x_ref, h_ref, *refs):
    out_refs = refs[-2:]
    for slot in (0, 1):
        mine = refs[2 * early * slot : 2 * early * (slot + 1)]
        for pair, act_ref, moved in ((0, x_ref, mine[:early]), (1, h_ref, mine[early:])):
            total = kernel_sums([act_ref.at[slot, n] for n in range(early)], moved, extent)
            for row, value in pieces(total, pair):
                out_refs[slot][row : row + PIECE, :] = value


def even_last_kernel(extent, early, x_ref, h_ref, w_ref, g_ref, acc_ref, *refs):
    gx_ref, out_ref, mg_ref, mh_ref = refs
    gx_ref[...] = step(
        g_ref[...],
        x_ref.at[0, early],
        h_ref.at[0, early],
        w_ref.at[0],
        mg_ref,
        mh_ref,
        extent,
    )
    for pair, act_ref, moved_ref in ((0, x_ref, mh_ref), (1, h_ref, mg_ref)):
        total = kernel_sums([act_ref.at[0, early]], [moved_ref], extent)
        for row, value in pieces(total, pair):
            value = value + acc_ref[row : row + PIECE, :]
            out_ref[row : row + PIECE, :] = value.astype(BF16)


def last_kernel(extent, early, parts, x_ref, h_ref, w_ref, g_ref, loss_ref, *refs):
    gx0_ref, sums0_ref, acc_ref, edge_hbm, out_ref, mg_ref, mh_ref, gx1_ref, sems = refs
    position = lax.axis_index("section")
    parity = position & 1
    g = (g_ref[...].astype(F32) + loss_ref[early - 1].astype(F32)).astype(BF16)
    copies = [
        pltpu.make_async_copy(gx0_ref, edge_hbm.at[parity], sems.at[0]),
        pltpu.make_async_copy(gx1_ref, edge_hbm.at[1 - parity], sems.at[1]),
    ]
    copies[0].start()
    members, _, later, rows_each, _ = out_ref.shape
    upper = (position >= lax.axis_size("section") // 2).astype(jnp.int32)
    half0, half1 = (parity + upper) & 1, (1 - parity + upper) & 1

    def put(row, half, value):
        shard, inner = row // rows_each, row % rows_each
        block, pair_at = shard // (2 * later), shard % (2 * later)
        member = block * (members // parts) + pair_at % 2
        out_ref[member, half, pair_at // 2, inner : inner + value.shape[0], :] = value

    for row in range(0, sums0_ref.shape[0], rows_each):
        put(row, half0, sums0_ref[row : row + rows_each, :])
    gx1_ref[...] = step(
        g, x_ref.at[1, early], h_ref.at[1, early], w_ref.at[1], mg_ref, mh_ref, extent
    )
    copies[1].start()
    for pair, act_ref, moved_ref in ((0, x_ref, mh_ref), (1, h_ref, mg_ref)):
        total = kernel_sums([act_ref.at[1, early]], [moved_ref], extent)
        for row, value in pieces(total, pair):
            put(row, half1, (value + acc_ref[row : row + PIECE, :]).astype(BF16))
    for copy in copies:
        copy.wait()


def call(body, steps, in_specs, out_shape, scratch, args, hbm_outs=0):
    cells, channels = args[0].shape[-2:]
    return pl.pallas_call(
        body,
        in_specs=in_specs,
        out_specs=[in_hbm()] * hbm_outs + [vmem()] * (len(out_shape) - hbm_outs),
        out_shape=out_shape,
        scratch_shapes=scratch,
        compiler_params=PARAMS,
        cost_estimate=pl.CostEstimate(
            flops=4 * steps * cells * TAPS * channels * channels,
            bytes_accessed=1000000,
            transcendentals=0,
        ),
    )(*args)


def vmem():
    return pl.BlockSpec(memory_space=pltpu.VMEM)


def in_hbm():
    return pl.BlockSpec(memory_space=pltpu.HBM)


def exchange(value, offset):
    total = lax.axis_size("section")
    pairs = []
    for low in range(offset, total - 1, 2):
        pairs += [(low, low + 1), (low + 1, low)]
    return lax.ppermute(value, "section", pairs)


def on_device(factors, saved_x, saved_h, kernels, grad_in, loss_grads):
    return whole(factors, saved_x, saved_h, kernels, grad_in, loss_grads)


def whole(factors, saved_x, saved_h, kernels, grad_in, loss_grads):
    ticks = saved_x.shape[1]
    extent, channels = saved_x.shape[4], saved_x.shape[6]
    cells = extent * extent
    sections = lax.axis_size("section")
    outer, inner = factors
    later, shards = inner // 2, outer * inner
    rows = 2 * TAPS * channels
    field = (cells, channels)

    def shape(*lead, tail=field):
        return jax.ShapeDtypeStruct((*lead, *tail), BF16)

    moved = shape(tail=(cells, 3 * channels))
    scratch = [pltpu.VMEM(moved.shape, BF16)] * 2

    xs, hs, ws, loss, mg0, mg1, mh0, mh1, out0, out1 = call(
        functools.partial(first_kernel, extent, ticks),
        2,
        [in_hbm()] * 5,
        [
            shape(2, ticks),
            shape(2, ticks),
            shape(*kernels.shape[1:-2], tail=(channels, channels)),
            shape(ticks - 1),
            *[moved] * 4,
            *[shape()] * 2,
        ],
        [pltpu.VMEM((2, *field), BF16), pltpu.SemaphoreType.DMA((15,))],
        [
            pltpu.with_memory_space_constraint(value, pltpu.HBM)
            for value in (
                saved_x.reshape(-1, *field),
                saved_h.reshape(-1, *field),
                kernels[0],
                grad_in.reshape(-1, *field),
                loss_grads.reshape(-1, *field),
            )
        ],
    )
    mg, mh = [[mg0], [mg1]], [[mh0], [mh1]]
    for tick in range(1, ticks):
        far = exchange(out0, 1)
        near = exchange(out1, 0)
        if tick == ticks - 1:
            break
        mg0, mh0, out0 = call(
            functools.partial(middle_kernel, extent, 0, tick),
            1,
            [vmem()] * 4,
            [moved, moved, shape()],
            [],
            (xs, hs, ws, near),
        )
        mg1, mh1, out1 = call(
            functools.partial(middle_kernel, extent, 1, tick),
            1,
            [vmem()] * 5,
            [moved, moved, shape()],
            [],
            (xs, hs, ws, far, loss),
        )
        for slot, used, made in ((0, mg0, mh0), (1, mg1, mh1)):
            mg[slot].append(used)
            mh[slot].append(made)
    early = ticks - 1
    sums = jax.ShapeDtypeStruct((rows, channels), F32)
    acc0, acc1 = call(
        functools.partial(early_kernel, extent, early),
        2 * early,
        [vmem()] * (2 + 4 * early),
        [sums, sums],
        [],
        (xs, hs, *mh[0], *mg[0], *mh[1], *mg[1]),
    )
    out0, sums0 = call(
        functools.partial(even_last_kernel, extent, early),
        2,
        [vmem()] * 5,
        [shape(), shape(tail=(rows, channels))],
        scratch,
        (xs, hs, ws, near, acc0),
    )
    edge, both = call(
        functools.partial(last_kernel, extent, early, outer),
        2,
        [vmem()] * 8,
        [shape(2), shape(2 * outer, 2, later, rows // shards, tail=(channels,))],
        [*scratch, pltpu.VMEM(field, BF16), pltpu.SemaphoreType.DMA((2,))],
        (xs, hs, ws, far, loss, out0, sums0, acc1),
        hbm_outs=1,
    )
    edge_grads = edge.reshape(2, 1, 1, extent, extent, channels)

    def shard(block, far, near):
        return (block * later + far) * 2 + near

    first_groups = [
        [shard(block, far, near) for block in range(outer) for near in range(2)]
        for far in range(later)
    ]
    second_groups = [
        [
            section * shards + shard(block, far, near)
            for section in (low, sections - 1 - low)
            for far in range(later)
        ]
        for low in range(sections // 2)
        for block in range(outer)
        for near in range(2)
    ]

    def total(value):
        parts = [value[n].astype(F32) for n in range(value.shape[0])]
        return functools.reduce(lambda a, b: a + b, parts)

    both = lax.all_to_all(both, "dp", 0, 0, axis_index_groups=first_groups, tiled=True)
    both = total(both).astype(BF16).reshape(2 * later, rows // shards, channels)
    both = lax.all_to_all(
        both, ("section", "dp"), 0, 0, axis_index_groups=second_groups, tiled=True
    )
    kernel_grads = (total(both) * (1.0 / float(cells)))[None]
    return (kernel_grads, edge_grads)


def solution(mesh):
    shards = mesh.shape["dp"]
    outer = next(f for f in (4, 2, 1) if shards % f == 0)
    return jax.shard_map(
        functools.partial(on_device, (outer, shards // outer)),
        mesh=mesh,
        in_specs=(
            P(None, None, "section", "dp", None, None, None),
            P(None, None, "section", "dp", None, None, None),
            P("section", None, None, None, None, None),
            P(None, "section", "dp", None, None, None),
            P(None, None, "dp", None, None, None),
        ),
        out_specs=(P("section", "dp", None), P(None, "section", "dp", None, None, None)),
        check_vma=False,
    )
```

```python
import functools

import jax
import jax.numpy as jnp
from jax import lax
from jax.experimental import pallas as pl
from jax.experimental.pallas import tpu as pltpu
from jax.sharding import PartitionSpec as P


TAPS = 9
PIECE = 16
PARAMS = pltpu.CompilerParams(vmem_limit_bytes=16 << 20)
BF16, F32 = jnp.bfloat16, jnp.float32


def moved_along_x(value, extent):
    cells, channels = value.shape
    wide = value.astype(F32)
    column = lax.broadcasted_iota(jnp.int32, (cells, channels), 0) & (extent - 1)
    left = jnp.where(column == extent - 1, 0.0, pltpu.roll(wide, cells - 1, 0))
    right = jnp.where(column == 0, 0.0, pltpu.roll(wide, 1, 0))
    return jnp.concatenate([left.astype(value.dtype), value, right.astype(value.dtype)], axis=1)


def down(value, extent):
    return jnp.concatenate([jnp.zeros_like(value[:extent]), value[:-extent]], axis=0)


def up(value, extent):
    return jnp.concatenate([value[extent:], jnp.zeros_like(value[:extent])], axis=0)


def conv_back(moved, w_ref, extent):
    rows = [jnp.concatenate([w_ref[3 * r + c] for c in range(3)], axis=1) for r in range(3)]
    result = lax.dot_general(
        moved,
        jnp.concatenate(rows, axis=0),
        (((1,), (1,)), ((), ())),
        preferred_element_type=F32,
    )
    above, level, below = jnp.split(result, 3, axis=1)
    return level + down(below, extent) + up(above, extent)


def step(g, x_ref, h_ref, w_ref, mg_ref, mh_ref, extent, between=None):
    mg_ref[...] = moved_along_x(g, extent)
    grad_z = conv_back(mg_ref[...], w_ref.at[1], extent)
    grad_h = jnp.where(h_ref[...].astype(F32) > 0, grad_z, 0.0).astype(BF16)
    mh_ref[...] = moved_along_x(grad_h, extent)
    if between is not None:
        between()
    grad_u = conv_back(mh_ref[...], w_ref.at[0], extent)
    passed = jnp.where(x_ref[...].astype(F32) > 0, grad_u, 0.0)
    return (g.astype(F32) + passed).astype(BF16)


def kernel_sums(act_refs, moved_refs, extent):
    rows = []
    for act_ref in act_refs:
        act = jnp.maximum(act_ref[...].astype(F32), 0.0).astype(BF16)
        rows.append(jnp.concatenate([down(act, extent), act, up(act, extent)], axis=1))
    return lax.dot_general(
        jnp.concatenate(rows, axis=0),
        jnp.concatenate([moved[...] for moved in moved_refs], axis=0),
        (((0,), (0,)), ((), ())),
        preferred_element_type=F32,
    )


def pieces(total, pair):
    channels = total.shape[0] // 3
    for k in range(TAPS):
        for start in range(0, channels, PIECE):
            top, left = k // 3 * channels + start, k % 3 * channels
            values = total[top : top + PIECE, left : left + channels]
            yield (pair * TAPS + k) * channels + start, values


def first_kernel(extent, ticks, x_hbm, h_hbm, w_hbm, g_hbm, l_hbm, *refs):
    xs, hs, ws, loss, mg0, mg1, mh0, mh1, gx0, gx1, gs, sems = refs
    position = lax.axis_index("section")
    parity = position & 1
    at_end = (position == 0) | (position == lax.axis_size("section") - 1)
    copies = []

    def fetch(source, target):
        copy = pltpu.make_async_copy(source, target, sems.at[len(copies)])
        copy.start()
        copies.append(copy)

    for slot in (0, 1):
        replica = parity if slot == 0 else 1 - parity
        fetch(g_hbm.at[replica], gs.at[slot])
        fetch(w_hbm.at[replica, 1], ws.at[slot, 1])
        fetch(h_hbm.at[replica * ticks], hs.at[slot, 0])
        fetch(w_hbm.at[replica, 0], ws.at[slot, 0])
        fetch(x_hbm.at[replica * ticks], xs.at[slot, 0])
    for slot in (0, 1):
        replica = parity if slot == 0 else 1 - parity
        later = pl.ds(replica * ticks + 1, ticks - 1)
        fetch(h_hbm.at[later], hs.at[slot, pl.ds(1, ticks - 1)])
        fetch(x_hbm.at[later], xs.at[slot, pl.ds(1, ticks - 1)])
    fetch(l_hbm.at[pl.ds((1 - parity) * (ticks - 1), ticks - 1)], loss)

    def wait(first, last):
        for copy in copies[first:last]:
            copy.wait()

    wait(0, 3)
    gx0[...] = step(
        gs[0], xs.at[0, 0], hs.at[0, 0], ws.at[0], mg0, mh0, extent, lambda: wait(3, 5)
    )
    wait(5, 8)
    gx1[...] = step(
        gs[1], xs.at[1, 0], hs.at[1, 0], ws.at[1], mg1, mh1, extent, lambda: wait(8, 10)
    )
    wait(10, len(copies))

    @pl.when(jnp.logical_not(at_end))
    def _():
        loss[...] = jnp.zeros_like(loss)


def middle_kernel(extent, slot, tick, x_ref, h_ref, w_ref, g_ref, *refs):
    g = g_ref[...]
    if slot == 1:
        g = (g.astype(F32) + refs[0][tick - 1].astype(F32)).astype(BF16)
    mg_ref, mh_ref, gx_ref = refs[-3:]
    gx_ref[...] = step(
        g, x_ref.at[slot, tick], h_ref.at[slot, tick], w_ref.at[slot], mg_ref, mh_ref, extent
    )


def early_kernel(extent, early, x_ref, h_ref, *refs):
    out_refs = refs[-2:]
    for slot in (0, 1):
        mine = refs[2 * early * slot : 2 * early * (slot + 1)]
        for pair, act_ref, moved in ((0, x_ref, mine[:early]), (1, h_ref, mine[early:])):
            total = kernel_sums([act_ref.at[slot, n] for n in range(early)], moved, extent)
            for row, value in pieces(total, pair):
                out_refs[slot][row : row + PIECE, :] = value


def even_last_kernel(extent, early, x_ref, h_ref, w_ref, g_ref, acc_ref, *refs):
    gx_ref, out_ref, mg_ref, mh_ref = refs
    gx_ref[...] = step(
        g_ref[...],
        x_ref.at[0, early],
        h_ref.at[0, early],
        w_ref.at[0],
        mg_ref,
        mh_ref,
        extent,
    )
    for pair, act_ref, moved_ref in ((0, x_ref, mh_ref), (1, h_ref, mg_ref)):
        total = kernel_sums([act_ref.at[0, early]], [moved_ref], extent)
        for row, value in pieces(total, pair):
            value = value + acc_ref[row : row + PIECE, :]
            out_ref[row : row + PIECE, :] = value.astype(BF16)


def last_kernel(extent, early, parts, x_ref, h_ref, w_ref, g_ref, loss_ref, *refs):
    sums0_ref, acc_ref, gx1_ref, out_ref, mg_ref, mh_ref = refs
    position = lax.axis_index("section")
    parity = position & 1
    g = (g_ref[...].astype(F32) + loss_ref[early - 1].astype(F32)).astype(BF16)
    members, _, later, rows_each, _ = out_ref.shape
    upper = (position >= lax.axis_size("section") // 2).astype(jnp.int32)
    half0, half1 = (parity + upper) & 1, (1 - parity + upper) & 1

    def put(row, half, value):
        shard, inner = row // rows_each, row % rows_each
        block, pair_at = shard // (2 * later), shard % (2 * later)
        member = block * (members // parts) + pair_at % 2
        out_ref[member, half, pair_at // 2, inner : inner + value.shape[0], :] = value

    for row in range(0, sums0_ref.shape[0], rows_each):
        put(row, half0, sums0_ref[row : row + rows_each, :])
    gx1_ref[...] = step(
        g, x_ref.at[1, early], h_ref.at[1, early], w_ref.at[1], mg_ref, mh_ref, extent
    )
    for pair, act_ref, moved_ref in ((0, x_ref, mh_ref), (1, h_ref, mg_ref)):
        total = kernel_sums([act_ref.at[1, early]], [moved_ref], extent)
        for row, value in pieces(total, pair):
            put(row, half1, (value + acc_ref[row : row + PIECE, :]).astype(BF16))


def finish_kernel(factor, parts_ref, gx0_ref, gx1_ref, sum_ref, edge_ref):
    parity = lax.axis_index("section") & 1
    edge_ref[parity] = gx0_ref[...]
    edge_ref[1 - parity] = gx1_ref[...]
    total = parts_ref[0].astype(F32)
    for n in range(1, parts_ref.shape[0]):
        total = total + parts_ref[n].astype(F32)
    sum_ref[...] = total * factor


def call(body, steps, in_specs, out_shape, scratch, args):
    cells, channels = args[0].shape[-2:]
    return pl.pallas_call(
        body,
        in_specs=in_specs,
        out_specs=[vmem()] * len(out_shape),
        out_shape=out_shape,
        scratch_shapes=scratch,
        compiler_params=PARAMS,
        cost_estimate=pl.CostEstimate(
            flops=4 * steps * cells * TAPS * channels * channels,
            bytes_accessed=1000000,
            transcendentals=0,
        ),
    )(*args)


def vmem():
    return pl.BlockSpec(memory_space=pltpu.VMEM)


def in_hbm():
    return pl.BlockSpec(memory_space=pltpu.HBM)


def exchange(value, offset):
    total = lax.axis_size("section")
    pairs = []
    for low in range(offset, total - 1, 2):
        pairs += [(low, low + 1), (low + 1, low)]
    return lax.ppermute(value, "section", pairs)


def on_device(factors, saved_x, saved_h, kernels, grad_in, loss_grads):
    return whole(factors, saved_x, saved_h, kernels, grad_in, loss_grads)


def whole(factors, saved_x, saved_h, kernels, grad_in, loss_grads):
    ticks = saved_x.shape[1]
    extent, channels = saved_x.shape[4], saved_x.shape[6]
    cells = extent * extent
    sections = lax.axis_size("section")
    outer, inner = factors
    later, shards = inner // 2, outer * inner
    rows = 2 * TAPS * channels
    field = (cells, channels)

    def shape(*lead, tail=field):
        return jax.ShapeDtypeStruct((*lead, *tail), BF16)

    moved = shape(tail=(cells, 3 * channels))
    scratch = [pltpu.VMEM(moved.shape, BF16)] * 2

    xs, hs, ws, loss, mg0, mg1, mh0, mh1, out0, out1 = call(
        functools.partial(first_kernel, extent, ticks),
        2,
        [in_hbm()] * 5,
        [
            shape(2, ticks),
            shape(2, ticks),
            shape(*kernels.shape[1:-2], tail=(channels, channels)),
            shape(ticks - 1),
            *[moved] * 4,
            *[shape()] * 2,
        ],
        [pltpu.VMEM((2, *field), BF16), pltpu.SemaphoreType.DMA((15,))],
        [
            pltpu.with_memory_space_constraint(value, pltpu.HBM)
            for value in (
                saved_x.reshape(-1, *field),
                saved_h.reshape(-1, *field),
                kernels[0],
                grad_in.reshape(-1, *field),
                loss_grads.reshape(-1, *field),
            )
        ],
    )
    mg, mh = [[mg0], [mg1]], [[mh0], [mh1]]
    for tick in range(1, ticks):
        far = exchange(out0, 1)
        near = exchange(out1, 0)
        if tick == ticks - 1:
            break
        mg0, mh0, out0 = call(
            functools.partial(middle_kernel, extent, 0, tick),
            1,
            [vmem()] * 4,
            [moved, moved, shape()],
            [],
            (xs, hs, ws, near),
        )
        mg1, mh1, out1 = call(
            functools.partial(middle_kernel, extent, 1, tick),
            1,
            [vmem()] * 5,
            [moved, moved, shape()],
            [],
            (xs, hs, ws, far, loss),
        )
        for slot, used, made in ((0, mg0, mh0), (1, mg1, mh1)):
            mg[slot].append(used)
            mh[slot].append(made)
    early = ticks - 1
    sums = jax.ShapeDtypeStruct((rows, channels), F32)
    acc0, acc1 = call(
        functools.partial(early_kernel, extent, early),
        2 * early,
        [vmem()] * (2 + 4 * early),
        [sums, sums],
        [],
        (xs, hs, *mh[0], *mg[0], *mh[1], *mg[1]),
    )
    out0, sums0 = call(
        functools.partial(even_last_kernel, extent, early),
        2,
        [vmem()] * 5,
        [shape(), shape(tail=(rows, channels))],
        scratch,
        (xs, hs, ws, near, acc0),
    )
    out1, both = call(
        functools.partial(last_kernel, extent, early, outer),
        2,
        [vmem()] * 7,
        [shape(), shape(2 * outer, 2, later, rows // shards, tail=(channels,))],
        scratch,
        (xs, hs, ws, far, loss, sums0, acc1),
    )

    def shard(block, far, near):
        return (block * later + far) * 2 + near

    first_groups = [
        [shard(block, far, near) for block in range(outer) for near in range(2)]
        for far in range(later)
    ]
    second_groups = [
        [
            section * shards + shard(block, far, near)
            for section in (low, sections - 1 - low)
            for far in range(later)
        ]
        for low in range(sections // 2)
        for block in range(outer)
        for near in range(2)
    ]

    def total(value):
        parts = [value[n].astype(F32) for n in range(value.shape[0])]
        return functools.reduce(lambda a, b: a + b, parts)

    both = lax.all_to_all(both, "dp", 0, 0, axis_index_groups=first_groups, tiled=True)
    both = total(both).astype(BF16).reshape(2 * later, rows // shards, channels)
    both = lax.all_to_all(
        both, ("section", "dp"), 0, 0, axis_index_groups=second_groups, tiled=True
    )
    kernel_grads, edge = call(
        functools.partial(finish_kernel, 1.0 / float(cells)),
        0,
        [vmem()] * 3,
        [jax.ShapeDtypeStruct((rows // shards, channels), F32), shape(2)],
        [],
        (both, out0, out1),
    )
    return (kernel_grads[None], edge.reshape(2, 1, 1, extent, extent, channels))


def solution(mesh):
    shards = mesh.shape["dp"]
    outer = next(f for f in (4, 2, 1) if shards % f == 0)
    return jax.shard_map(
        functools.partial(on_device, (outer, shards // outer)),
        mesh=mesh,
        in_specs=(
            P(None, None, "section", "dp", None, None, None),
            P(None, None, "section", "dp", None, None, None),
            P("section", None, None, None, None, None),
            P(None, "section", "dp", None, None, None),
            P(None, None, "dp", None, None, None),
        ),
        out_specs=(P("section", "dp", None), P(None, "section", "dp", None, None, None)),
        check_vma=False,
    )
```
